256 devices in a mesh: seq: 64 (over x, z, core), head: 4 (over y).
Axes of the slice: x: 4, y: 4, z: 8, core: 2. Of those that a mesh axis runs over, the one named last changes fastest.
Arguments:
- queries: bfloat16 [16384, 4096], P('seq', 'head'), may hold values from -4 to 4
- key_rows: bfloat16 [16384, 4096], P('seq', 'head'), may hold values from -4 to 4
- value_rows: bfloat16 [16384, 4096], P('seq', 'head'), may hold values from -28 to 28
- norm_gain: float32 [4096], P('head'), may hold values from 0.1 to 1.9
- out_grad: bfloat16 [16384, 4096], P('seq', 'head'), may hold values from -4 to 4
Outputs:
- normed: bfloat16 [16384, 4096], P('seq', 'head')
- query_grad: bfloat16 [16384, 4096], P('seq', 'head')
- key_grad: bfloat16 [16384, 4096], P('seq', 'head')
- value_grad: bfloat16 [16384, 4096], P('seq', 'head')
The draws below stay inside these ranges and needn't reach their ends.
All inputs are finite; a program needn't handle non-finite values.
Results may differ from the reference program's by a relative error of at most 0.0017.
The reference program's roundings to bfloat16 on the way (of `query_feat`, `key_feat`, `scores_low`, `numer_low` and `mixed_low`) count: a program that leaves them out, or rounds other values in their place, can miss the bound.
Values sent between devices are 32-bit elements; how exact they have to be, the bound alone decides.
No kernel may reach another device: no remote copies, remote signals or barrier semaphores. Data moves between devices by JAX's collectives and lax.ppermute only.
A program may use at most 192 MiB of HBM per device.

```python
import jax
import jax.numpy as jnp
from jax import lax

HEADS = 32
HEAD_DIM = 128
TOK_DEV = 256
D = 4096
TOKENS = 16384
N_SEQ = 64


def draw_value_rows(key, part):
    first = jax.random.fold_in(key, 0)
    column = jnp.arange(D, dtype=jnp.float32) / (D - 1)
    base = jnp.clip(jax.random.normal(first, (TOKENS, D), jnp.float32), -4.0, 4.0)
    return (base * jnp.exp(0.5 * column * jnp.log(3.0))).astype(jnp.bfloat16)


def levels(key, dims, cuts, smallest, high):
    level = 1.0
    for dim, parts in cuts:
        steps = jax.random.uniform(jax.random.fold_in(jax.random.fold_in(key, 6), dim), (parts,), jnp.float32, smallest / len(cuts), high / len(cuts))
        level = level * jnp.repeat(jnp.exp(steps), dims[dim] // parts).reshape((-1,) + (1,) * (len(dims) - 1 - dim))
    return level


def scatter_about(key, shape, scale, bound, pieces=(), kind=jnp.bfloat16):
    level = levels(key, shape, pieces, -0.22, 0.18) if pieces else 1.0
    drawn = jax.random.normal(key, shape, jnp.float32) * scale * level
    return jnp.minimum(jnp.maximum(drawn, -bound), bound).astype(kind)


def setup_inputs(seed: int = 0) -> dict:
    key_list = jax.random.split(jax.random.key(seed), 6)
    return {
        "queries": scatter_about(key_list[0], (TOKENS, D), 1.0, 4.0, ((0, 64), (1, 4))),
        "key_rows": scatter_about(key_list[1], (TOKENS, D), 1.0, 4.0, ((0, 64), (1, 4))),
        "value_rows": draw_value_rows(jax.random.fold_in(key_list[5], 71), 0),
        "norm_gain": jnp.clip(1.0 + 0.18 * jax.random.normal(key_list[3], (D,), jnp.float32), 0.1, 1.9),
        "out_grad": scatter_about(key_list[4], (TOKENS, D), 1.0, 4.0, ((0, 64), (1, 4))),
    }


highest = lax.Precision.HIGHEST

def feature(values):
    return jnp.where(values > 0, values + 1.0, jnp.exp(jnp.minimum(values, 0.0)))

def feature_slope(values):
    return jnp.where(values > 0, jnp.ones_like(values), jnp.exp(jnp.minimum(values, 0.0)))

def round_low(values):
    return lax.optimization_barrier(values.astype(jnp.bfloat16)).astype(jnp.float32)

def to_blocks(array):
    return array.reshape(N_SEQ, TOK_DEV, HEADS, HEAD_DIM).transpose(0, 2, 1, 3)

def from_blocks(array):
    return array.transpose(0, 2, 1, 3).reshape(TOKENS, HEADS * HEAD_DIM)

def causal_mask():
    rows = lax.broadcasted_iota(jnp.int32, (TOK_DEV, TOK_DEV), 0)
    cols = lax.broadcasted_iota(jnp.int32, (TOK_DEV, TOK_DEV), 1)
    return (rows >= cols)[None]

def block_scores(query32, key32, mask):
    scores = jnp.einsum('hte,hse->hts', query32, key32, precision=highest)
    return jnp.where(mask, scores, 0.0)

def reference(queries, key_rows, value_rows, norm_gain, out_grad):
    width = HEADS * HEAD_DIM
    query_feat = feature(queries.astype(jnp.float32)).astype(jnp.bfloat16)
    key_feat = feature(key_rows.astype(jnp.float32)).astype(jnp.bfloat16)
    query_blocks = to_blocks(query_feat)
    key_blocks = to_blocks(key_feat)
    value_blocks = to_blocks(value_rows)
    mask = causal_mask()

    def forward_block(carry, block):
        prefix_kv, prefix_ks = carry
        query_blk, key_blk, value_blk = block
        query32 = query_blk.astype(jnp.float32)
        key32 = key_blk.astype(jnp.float32)
        value32 = value_blk.astype(jnp.float32)
        scores = block_scores(query32, key32, mask)
        scores_low = round_low(scores)
        numer = jnp.einsum('hte,hef->htf', query32, prefix_kv, precision=highest)
        numer = numer + jnp.einsum('hts,hsf->htf', scores_low, value32, precision=highest)
        denom = jnp.einsum('hte,he->ht', query32, prefix_ks, precision=highest) + lax.optimization_barrier(jnp.sum(scores, axis=2))
        attn = numer / denom[:, :, None]
        block_kv = jnp.einsum('hse,hsf->hef', key32, value32, precision=highest)
        block_ks = lax.optimization_barrier(jnp.sum(key32, axis=1))
        return ((prefix_kv + block_kv, prefix_ks + block_ks), (attn, denom, prefix_kv, prefix_ks))
    start = (jnp.zeros((HEADS, HEAD_DIM, HEAD_DIM), jnp.float32), jnp.zeros((HEADS, HEAD_DIM), jnp.float32))
    _, (attn, denom, prefix_kv, prefix_ks) = lax.scan(forward_block, start, (query_blocks, key_blocks, value_blocks))
    gain = norm_gain.astype(jnp.float32).reshape(1, HEADS, 1, HEAD_DIM)
    inv_rms = lax.rsqrt(lax.optimization_barrier(jnp.sum(attn * attn, axis=(1, 3))) / width + 1e-06)
    normed = from_blocks(gain * attn * inv_rms[:, None, :, None]).astype(jnp.bfloat16)
    grad_blocks = to_blocks(out_grad)
    cross = lax.optimization_barrier(jnp.sum(attn * (gain * grad_blocks.astype(jnp.float32)), axis=(1, 3))) / width
    raw_q = to_blocks(queries)
    raw_k = to_blocks(key_rows)
    gain_heads = norm_gain.astype(jnp.float32).reshape(HEADS, 1, HEAD_DIM)

    def backward_block(carry, block):
        suffix_g, suffix_gz = carry
        query_blk, key_blk, value_blk, attn_blk, denom_blk, prefix_kv_blk, prefix_ks_blk, grad_blk, inv_blk, cross_blk, query_raw, key_raw = block
        query32 = query_blk.astype(jnp.float32)
        key32 = key_blk.astype(jnp.float32)
        value32 = value_blk.astype(jnp.float32)
        scores = block_scores(query32, key32, mask)
        scores_low = round_low(scores)
        grad_in = gain_heads * grad_blk.astype(jnp.float32)
        scale = inv_blk[None, :, None]
        d_attn = scale * grad_in - attn_blk * scale ** 3 * cross_blk[None, :, None]
        d_numer = d_attn / denom_blk[:, :, None]
        d_denom = -lax.optimization_barrier(jnp.sum(d_attn * attn_blk, axis=2)) / denom_blk
        numer_low = round_low(d_numer)
        mixed = jnp.einsum('htf,hsf->hts', numer_low, value32, precision=highest) + d_denom[:, :, None]
        mixed_low = round_low(jnp.where(mask, mixed, 0.0))
        q_grad = jnp.einsum('htf,hef->hte', d_numer, prefix_kv_blk, precision=highest)
        q_grad = q_grad + d_denom[:, :, None] * prefix_ks_blk[:, None, :]
        q_grad = q_grad + jnp.einsum('hts,hse->hte', mixed_low, key32, precision=highest)
        k_grad = jnp.einsum('hsf,hef->hse', value32, suffix_g, precision=highest) + suffix_gz[:, None, :]
        k_grad = k_grad + jnp.einsum('hts,hte->hse', mixed_low, query32, precision=highest)
        v_grad = jnp.einsum('hse,hef->hsf', key32, suffix_g, precision=highest)
        v_grad = v_grad + jnp.einsum('hts,htf->hsf', scores_low, numer_low, precision=highest)
        block_g = jnp.einsum('hte,htf->hef', query32, numer_low, precision=highest)
        block_gz = jnp.einsum('hte,ht->he', query32, d_denom, precision=highest)
        q_out = (q_grad * feature_slope(query_raw.astype(jnp.float32))).astype(jnp.bfloat16)
        k_out = (k_grad * feature_slope(key_raw.astype(jnp.float32))).astype(jnp.bfloat16)
        return ((suffix_g + block_g, suffix_gz + block_gz), (q_out, k_out, v_grad.astype(jnp.bfloat16)))
    _, (q_blocks, k_blocks, v_blocks) = lax.scan(backward_block, start, (query_blocks, key_blocks, value_blocks, attn, denom, prefix_kv, prefix_ks, grad_blocks, inv_rms, cross, raw_q, raw_k), reverse=True)
    return (normed, from_blocks(q_blocks), from_blocks(k_blocks), from_blocks(v_blocks))
```

```python
import jax
import jax.numpy as jnp
from jax import lax
from jax.sharding import Mesh
from jax.sharding import PartitionSpec as P

HEADS = 32
HEAD_DIM = 128
CORES = 2
ROWS = 16

highest = lax.Precision.HIGHEST


def feature(values):
    return jnp.where(values > 0, values + 1.0, jnp.exp(jnp.minimum(values, 0.0)))


def feature_slope(values):
    return jnp.where(values > 0, jnp.ones_like(values), jnp.exp(jnp.minimum(values, 0.0)))


def swap_cores(array):
    return lax.ppermute(array, "core", [(0, 1), (1, 0)])


def to_wire(state, row, chips):
    half = state.shape[0] // CORES
    state = state.reshape(CORES, chips, ROWS, HEAD_DIM)
    row = row.reshape(CORES, half, 1, 1, HEAD_DIM)
    row = jnp.pad(row, ((0, 0), (0, 0), (0, chips // half - 1), (0, 0), (0, 0)))
    return jnp.concatenate([state, row.reshape(CORES, chips, 1, HEAD_DIM)], axis=2)


def from_wire(wire, heads):
    chips = wire.shape[1]
    state = wire[:, :, :ROWS].reshape(heads, HEAD_DIM, HEAD_DIM)
    row = wire[:, :, ROWS].reshape(heads, (chips * CORES) // heads, HEAD_DIM)[:, 0]
    return state, row


def scan_states(state, row, backward):
    chips = lax.axis_size("chip")
    core = lax.axis_index("core")
    heads = state.shape[0]
    mine = to_wire(state, row, chips)
    other = swap_cores(mine)
    pair = lax.dynamic_index_in_dim(mine + other, core, 0, False)
    spread = lax.all_to_all(pair, "chip", 0, 0)
    order = range(chips - 1, -1, -1) if backward else range(chips)
    total = jnp.zeros_like(spread[0])
    sums = [None] * chips
    for chip in order:
        sums[chip] = total
        total = total + spread[chip]
    kept = lax.all_to_all(jnp.stack(sums), "chip", 0, 0)
    got = swap_cores(kept)
    first = jnp.where(core == 0, kept, got)
    second = jnp.where(core == 0, got, kept)
    adds = (core == 0) if backward else (core == 1)
    out = jnp.stack([first, second]) + jnp.where(adds, other, 0.0)
    return from_wire(out, heads)


def heads_major(array, heads_here):
    return array.reshape(array.shape[0], heads_here, HEAD_DIM).transpose(1, 0, 2)


def tokens_major(array):
    return array.transpose(1, 0, 2).reshape(array.shape[1], -1)


def body(queries, key_rows, value_rows, norm_gain, out_grad):
    width = HEADS * HEAD_DIM
    tokens = queries.shape[0]
    heads_here = norm_gain.shape[0] // HEAD_DIM
    query_raw = heads_major(queries, heads_here).astype(jnp.float32)
    key_raw = heads_major(key_rows, heads_here).astype(jnp.float32)
    query_feat = feature(query_raw).astype(jnp.bfloat16)
    key_feat = feature(key_raw).astype(jnp.bfloat16)
    value_in = heads_major(value_rows, heads_here)
    query32 = query_feat.astype(jnp.float32)
    key32 = key_feat.astype(jnp.float32)
    value32 = value_in.astype(jnp.float32)
    rows = lax.broadcasted_iota(jnp.int32, (tokens, tokens), 0)
    cols = lax.broadcasted_iota(jnp.int32, (tokens, tokens), 1)
    mask = (rows >= cols)[None]
    scores = jnp.einsum("hte,hse->hts", query_feat, key_feat, preferred_element_type=jnp.float32)
    scores = jnp.where(mask, scores, 0.0)
    scores_low = scores.astype(jnp.bfloat16)
    block_kv = jnp.einsum("hse,hsf->hef", key_feat, value_in, preferred_element_type=jnp.float32)
    block_ks = jnp.sum(key32, axis=1)
    prefix_kv, prefix_ks = scan_states(block_kv, block_ks, False)
    numer = jnp.einsum("hte,hef->htf", query32, prefix_kv, precision=highest)
    numer = numer + jnp.einsum(
        "hts,hsf->htf", scores_low, value_in, preferred_element_type=jnp.float32
    )
    denom = jnp.einsum("hte,he->ht", query32, prefix_ks, precision=highest) + jnp.sum(
        scores, axis=2
    )
    attn = numer / denom[:, :, None]
    gain = norm_gain.reshape(heads_here, 1, HEAD_DIM)
    grad_in = gain * heads_major(out_grad, heads_here).astype(jnp.float32)
    sum_squares, cross = lax.psum(
        (jnp.sum(attn * attn, axis=(0, 2)), jnp.sum(attn * grad_in, axis=(0, 2))), "head"
    )
    inv_rms = lax.rsqrt(sum_squares / width + 1e-06)[None, :, None]
    normed = tokens_major((gain * attn * inv_rms).astype(jnp.bfloat16))
    d_attn = inv_rms * grad_in - attn * inv_rms**3 * (cross / width)[None, :, None]
    d_numer = d_attn / denom[:, :, None]
    d_denom = -jnp.sum(d_attn * attn, axis=2) / denom
    numer_low = d_numer.astype(jnp.bfloat16)
    mixed = jnp.einsum("htf,hsf->hts", numer_low, value_in, preferred_element_type=jnp.float32)
    mixed = jnp.where(mask, mixed + d_denom[:, :, None], 0.0)
    mixed_low = mixed.astype(jnp.bfloat16)
    block_g = jnp.einsum("hte,htf->hef", query_feat, numer_low, preferred_element_type=jnp.float32)
    block_gz = jnp.einsum("hte,ht->he", query32, d_denom, precision=highest)
    suffix_g, suffix_gz = scan_states(block_g, block_gz, True)
    q_grad = jnp.einsum("htf,hef->hte", d_numer, prefix_kv, precision=highest)
    q_grad = q_grad + d_denom[:, :, None] * prefix_ks[:, None, :]
    q_grad = q_grad + jnp.einsum(
        "hts,hse->hte", mixed_low, key_feat, preferred_element_type=jnp.float32
    )
    k_grad = (
        jnp.einsum("hsf,hef->hse", value32, suffix_g, precision=highest) + suffix_gz[:, None, :]
    )
    k_grad = k_grad + jnp.einsum(
        "hts,hte->hse", mixed_low, query_feat, preferred_element_type=jnp.float32
    )
    v_grad = jnp.einsum("hse,hef->hsf", key32, suffix_g, precision=highest)
    v_grad = v_grad + jnp.einsum(
        "hts,htf->hsf", scores_low, numer_low, preferred_element_type=jnp.float32
    )
    query_grad = tokens_major((q_grad * feature_slope(query_raw)).astype(jnp.bfloat16))
    key_grad = tokens_major((k_grad * feature_slope(key_raw)).astype(jnp.bfloat16))
    value_grad = tokens_major(v_grad.astype(jnp.bfloat16))
    return (normed, query_grad, key_grad, value_grad)


def solution(mesh):
    devices = mesh.devices
    fine = Mesh(
        devices.reshape(devices.shape[0] // CORES, CORES, devices.shape[1]),
        ("chip", "core", "head"),
    )
    rows = P(("chip", "core"), "head")
    return jax.shard_map(
        body,
        mesh=fine,
        in_specs=(rows, rows, rows, P("head"), rows),
        out_specs=(rows, rows, rows, rows),
        check_vma=False,
    )
```

```python
import functools

import jax
import jax.numpy as jnp
from jax import lax
from jax.experimental import pallas as pl
from jax.experimental.pallas import tpu as pltpu
from jax.sharding import Mesh
from jax.sharding import PartitionSpec as P

HEADS = 32
HEAD_DIM = 128
CORES = 2
ROWS = 16

highest = lax.Precision.HIGHEST


def feature(values):
    return jnp.where(values > 0, values + 1.0, jnp.exp(jnp.minimum(values, 0.0)))


def feature_slope(values):
    return jnp.where(values > 0, jnp.ones_like(values), jnp.exp(jnp.minimum(values, 0.0)))


def swap_cores(array):
    return lax.ppermute(array, "core", [(0, 1), (1, 0)])


def to_wire(state, row, chips):
    half = state.shape[0] // CORES
    state = state.reshape(CORES, chips, ROWS, HEAD_DIM)
    row = row.reshape(CORES, half, 1, 1, HEAD_DIM)
    row = jnp.pad(row, ((0, 0), (0, 0), (0, chips // half - 1), (0, 0), (0, 0)))
    return jnp.concatenate([state, row.reshape(CORES, chips, 1, HEAD_DIM)], axis=2)


def from_wire(wire, heads):
    chips = wire.shape[1]
    state = wire[:, :, :ROWS].reshape(heads, HEAD_DIM, HEAD_DIM)
    row = wire[:, :, ROWS].reshape(heads, (chips * CORES) // heads, HEAD_DIM)[:, 0]
    return state, row


def chip_sums_kernel(backward, spread, sums):
    chips = spread.shape[0]
    total = jnp.zeros(spread.shape[1:], jnp.float32)
    for step in range(chips):
        chip = chips - 1 - step if backward else step
        sums[chip] = total
        if step < chips - 1:
            total = total + spread[chip]


def chip_sums(spread, backward):
    return pl.pallas_call(
        functools.partial(chip_sums_kernel, backward),
        out_shape=jax.ShapeDtypeStruct(spread.shape, jnp.float32),
        name="chip_sums",
    )(spread)


def scan_states(state, row, backward):
    chips = lax.axis_size("chip")
    core = lax.axis_index("core")
    heads = state.shape[0]
    mine = to_wire(state, row, chips)
    other = swap_cores(mine)
    pair = lax.dynamic_index_in_dim(mine + other, core, 0, False)
    spread = lax.all_to_all(pair, "chip", 0, 0)
    kept = lax.all_to_all(chip_sums(spread, backward), "chip", 0, 0)
    got = swap_cores(kept)
    first = jnp.where(core == 0, kept, got)
    second = jnp.where(core == 0, got, kept)
    adds = (core == 0) if backward else (core == 1)
    out = jnp.stack([first, second]) + jnp.where(adds, other, 0.0)
    return from_wire(out, heads)


def heads_major(array, heads_here):
    return array.reshape(array.shape[0], heads_here, HEAD_DIM).transpose(1, 0, 2)


def tokens_major(array):
    return array.transpose(1, 0, 2).reshape(array.shape[1], -1)


def body(queries, key_rows, value_rows, norm_gain, out_grad):
    width = HEADS * HEAD_DIM
    tokens = queries.shape[0]
    heads_here = norm_gain.shape[0] // HEAD_DIM
    query_raw = heads_major(queries, heads_here).astype(jnp.float32)
    key_raw = heads_major(key_rows, heads_here).astype(jnp.float32)
    query_feat = feature(query_raw).astype(jnp.bfloat16)
    key_feat = feature(key_raw).astype(jnp.bfloat16)
    value_in = heads_major(value_rows, heads_here)
    query32 = query_feat.astype(jnp.float32)
    key32 = key_feat.astype(jnp.float32)
    value32 = value_in.astype(jnp.float32)
    rows = lax.broadcasted_iota(jnp.int32, (tokens, tokens), 0)
    cols = lax.broadcasted_iota(jnp.int32, (tokens, tokens), 1)
    mask = (rows >= cols)[None]
    scores = jnp.einsum("hte,hse->hts", query_feat, key_feat, preferred_element_type=jnp.float32)
    scores = jnp.where(mask, scores, 0.0)
    scores_low = scores.astype(jnp.bfloat16)
    block_kv = jnp.einsum("hse,hsf->hef", key_feat, value_in, preferred_element_type=jnp.float32)
    block_ks = jnp.sum(key32, axis=1)
    prefix_kv, prefix_ks = scan_states(block_kv, block_ks, False)
    numer = jnp.einsum("hte,hef->htf", query32, prefix_kv, precision=highest)
    numer = numer + jnp.einsum(
        "hts,hsf->htf", scores_low, value_in, preferred_element_type=jnp.float32
    )
    denom = jnp.einsum("hte,he->ht", query32, prefix_ks, precision=highest) + jnp.sum(
        scores, axis=2
    )
    attn = numer / denom[:, :, None]
    gain = norm_gain.reshape(heads_here, 1, HEAD_DIM)
    grad_in = gain * heads_major(out_grad, heads_here).astype(jnp.float32)
    sum_squares, cross = lax.psum(
        (jnp.sum(attn * attn, axis=(0, 2)), jnp.sum(attn * grad_in, axis=(0, 2))), "head"
    )
    inv_rms = lax.rsqrt(sum_squares / width + 1e-06)[None, :, None]
    normed = tokens_major((gain * attn * inv_rms).astype(jnp.bfloat16))
    d_attn = inv_rms * grad_in - attn * inv_rms**3 * (cross / width)[None, :, None]
    d_numer = d_attn / denom[:, :, None]
    d_denom = -jnp.sum(d_attn * attn, axis=2) / denom
    numer_low = d_numer.astype(jnp.bfloat16)
    mixed = jnp.einsum("htf,hsf->hts", numer_low, value_in, preferred_element_type=jnp.float32)
    mixed = jnp.where(mask, mixed + d_denom[:, :, None], 0.0)
    mixed_low = mixed.astype(jnp.bfloat16)
    block_g = jnp.einsum("hte,htf->hef", query_feat, numer_low, preferred_element_type=jnp.float32)
    block_gz = jnp.einsum("hte,ht->he", query32, d_denom, precision=highest)
    suffix_g, suffix_gz = scan_states(block_g, block_gz, True)
    q_grad = jnp.einsum("htf,hef->hte", d_numer, prefix_kv, precision=highest)
    q_grad = q_grad + d_denom[:, :, None] * prefix_ks[:, None, :]
    q_grad = q_grad + jnp.einsum(
        "hts,hse->hte", mixed_low, key_feat, preferred_element_type=jnp.float32
    )
    k_grad = (
        jnp.einsum("hsf,hef->hse", value32, suffix_g, precision=highest) + suffix_gz[:, None, :]
    )
    k_grad = k_grad + jnp.einsum(
        "hts,hte->hse", mixed_low, query_feat, preferred_element_type=jnp.float32
    )
    v_grad = jnp.einsum("hse,hef->hsf", key32, suffix_g, precision=highest)
    v_grad = v_grad + jnp.einsum(
        "hts,htf->hsf", scores_low, numer_low, preferred_element_type=jnp.float32
    )
    query_grad = tokens_major((q_grad * feature_slope(query_raw)).astype(jnp.bfloat16))
    key_grad = tokens_major((k_grad * feature_slope(key_raw)).astype(jnp.bfloat16))
    value_grad = tokens_major(v_grad.astype(jnp.bfloat16))
    return (normed, query_grad, key_grad, value_grad)


def solution(mesh):
    devices = mesh.devices
    fine = Mesh(
        devices.reshape(devices.shape[0] // CORES, CORES, devices.shape[1]),
        ("chip", "core", "head"),
    )
    rows = P(("chip", "core"), "head")
    return jax.shard_map(
        body,
        mesh=fine,
        in_specs=(rows, rows, rows, P("head"), rows),
        out_specs=(rows, rows, rows, rows),
        check_vma=False,
    )
```

```python
import functools

import jax
import jax.numpy as jnp
from jax import lax
from jax.experimental import pallas as pl
from jax.experimental.pallas import tpu as pltpu
from jax.sharding import Mesh
from jax.sharding import PartitionSpec as P

HEADS = 32
HEAD_DIM = 128
CORES = 2
ROWS = 16
BLOCK = 256
BLOCKS = HEAD_DIM // ROWS

f32 = jnp.float32
bf16 = jnp.bfloat16
highest = lax.Precision.HIGHEST


def feature(values):
    return jnp.where(values > 0, values + 1.0, jnp.exp(jnp.minimum(values, 0.0)))


def feature_slope(values):
    return jnp.where(values > 0, jnp.ones_like(values), jnp.exp(jnp.minimum(values, 0.0)))


def dot(left, right, left_dim, right_dim, precision=None):
    return lax.dot_general(
        left,
        right,
        (((left_dim,), (right_dim,)), ((), ())),
        precision=precision,
        preferred_element_type=f32,
    )


def split(values):
    high = values.astype(bf16)
    return high, (values - high.astype(f32)).astype(bf16)


def head_columns(side, place, heads_side):
    return pl.ds(pl.multiple_of((side * heads_side + place) * HEAD_DIM, HEAD_DIM), HEAD_DIM)


def put_state(wire, place, state, row):
    first = place * BLOCKS
    wire[first : first + BLOCKS, 0:ROWS, :] = state.reshape(BLOCKS, ROWS, HEAD_DIM)
    wire[first : first + 1, ROWS : ROWS + 1, :] = row.reshape(1, 1, HEAD_DIM)


def clear_rows(wire):
    wire[:, ROWS : ROWS + 1, :] = jnp.zeros((wire.shape[0], 1, HEAD_DIM), f32)


def get_state(wire, extra, adds, place):
    first = place * BLOCKS
    blocks = pl.ds(first, BLOCKS)
    state = wire[blocks, 0:ROWS, :] + jnp.where(adds, extra[blocks, 0:ROWS, :], 0.0)
    row = wire[first, ROWS : ROWS + 1, :] + jnp.where(adds, extra[first, ROWS : ROWS + 1, :], 0.0)
    return state.reshape(HEAD_DIM, HEAD_DIM), row


def send_out(slots, target, slot, here, sem):
    copy = pltpu.make_async_copy(slots.at[slot], target.at[:, here], sem)
    copy.start()
    return copy


def causal(tokens):
    rows = lax.broadcasted_iota(jnp.int32, (tokens, tokens), 0)
    cols = lax.broadcasted_iota(jnp.int32, (tokens, tokens), 1)
    return rows >= cols


def head_order(core, heads_side):
    return [(side, place) for side in (1 - core, core) for place in range(heads_side)]


def states_kernel(core, keys, values, mine, theirs, key_slots, value_slots, sems):
    heads_side = keys.shape[1] // HEAD_DIM // CORES
    order = head_order(core[0], heads_side)
    copies = []
    for slot, (side, place) in enumerate(order):
        here = head_columns(side, place, heads_side)
        pair = (
            pltpu.make_async_copy(keys.at[:, here], key_slots.at[slot], sems.at[0, slot]),
            pltpu.make_async_copy(values.at[:, here], value_slots.at[slot], sems.at[1, slot]),
        )
        for copy in pair:
            copy.start()
        copies.append(pair)
    clear_rows(theirs)
    clear_rows(mine)
    for slot, (side, place) in enumerate(order):
        for copy in copies[slot]:
            copy.wait()
        key_feat = feature(key_slots[slot].astype(f32)).astype(bf16)
        row = jnp.sum(key_feat.astype(f32), axis=0, keepdims=True)
        wire = theirs if slot < heads_side else mine
        put_state(wire, place, dot(value_slots[slot], key_feat, 0, 0), row)


def inside_forward_kernel(queries, keys, values, query_out, key_out, low_out, numer, denom):
    tokens, width = queries.shape
    mask = causal(tokens)
    for head in range(width // HEAD_DIM):
        here = pl.ds(head * HEAD_DIM, HEAD_DIM)
        query_feat = feature(queries[:, here].astype(f32)).astype(bf16)
        key_feat = feature(keys[:, here].astype(f32)).astype(bf16)
        query_out[:, here] = query_feat
        key_out[:, here] = key_feat
        scores = jnp.where(mask, dot(query_feat, key_feat, 1, 1), 0.0)
        scores_low = scores.astype(bf16)
        low_out[:, pl.ds(head * tokens, tokens)] = scores_low
        numer[:, here] = dot(scores_low, values[:, here], 1, 0)
        total = jnp.sum(scores, axis=1, keepdims=True)
        denom[:, here] = jnp.broadcast_to(total, (tokens, HEAD_DIM))


def attention_kernel(
    core, query_feat, numer_in, denom_in, kept, got, extra, extra_got, gain, out_grad,
    attn_out, inverse_out, stats,
):
    tokens, width = query_feat.shape
    heads_side = width // HEAD_DIM // CORES
    adds = core[0] == 1
    squares = jnp.zeros((tokens, HEAD_DIM), f32)
    cross = jnp.zeros((tokens, HEAD_DIM), f32)
    for wire, more, side in ((kept, extra, core[0]), (got, extra_got, 1 - core[0])):
        for place in range(heads_side):
            here = head_columns(side, place, heads_side)
            state, row = get_state(wire, more, adds, place)
            both = jnp.concatenate([state, jnp.broadcast_to(row, state.shape)], axis=0)
            right = jnp.concatenate(split(both), axis=1)
            query = query_feat[:, here]
            product = dot(jnp.concatenate([query, query], axis=1), right, 1, 1)
            numer = numer_in[:, here] + product[:, :HEAD_DIM]
            inverse = 1.0 / (denom_in[:, here] + product[:, HEAD_DIM:])
            attn = numer * inverse
            grad_in = gain[:, here] * out_grad[:, here].astype(f32)
            squares = squares + attn * attn
            cross = cross + attn * grad_in
            attn_out[:, here] = attn
            inverse_out[:, here] = inverse
    ones = jnp.ones((8, HEAD_DIM), f32)
    which = lax.broadcasted_iota(jnp.int32, (8, tokens), 0)
    row_squares = dot(ones, squares, 1, 1, highest)
    row_cross = dot(ones, cross, 1, 1, highest)
    stats[...] = jnp.where(which == 0, row_squares, jnp.where(which == 1, row_cross, 0.0))


def token_scales(stats, width_all):
    tokens = stats.shape[1]
    squares = stats[0:1, :]
    cross = stats[1:2, :]
    scale = lax.rsqrt(squares / width_all + 1e-06)
    slope = scale * scale * scale * (cross / width_all)
    which = lax.broadcasted_iota(jnp.int32, (8, tokens), 0)
    rows = jnp.where(which == 0, scale, jnp.where(which == 1, slope, 0.0))
    pick = lax.broadcasted_iota(jnp.int32, (8, 2 * HEAD_DIM), 0) == (
        lax.broadcasted_iota(jnp.int32, (8, 2 * HEAD_DIM), 1) // HEAD_DIM
    )
    spread = dot(rows, pick.astype(f32), 0, 0, highest)
    return spread[:, :HEAD_DIM], spread[:, HEAD_DIM:]


def gradient_kernel(
    core, query_feat, attn_in, inverse_in, gain, out_grad, stats, numer_out, denom_out, mine, theirs
):
    width = query_feat.shape[1]
    heads_side = width // HEAD_DIM // CORES
    scale, slope = token_scales(stats[...], HEADS * HEAD_DIM)
    for wire, side in ((theirs, 1 - core[0]), (mine, core[0])):
        clear_rows(wire)
        for place in range(heads_side):
            here = head_columns(side, place, heads_side)
            attn = attn_in[:, here]
            inverse = inverse_in[:, here]
            grad_in = gain[:, here] * out_grad[:, here].astype(f32)
            d_attn = scale * grad_in - attn * slope
            d_numer = d_attn * inverse
            total = jnp.sum(d_attn * attn, axis=1, keepdims=True)
            d_denom = -total * inverse
            numer_out[:, here] = d_numer
            denom_out[:, here] = d_denom
            query = query_feat[:, here]
            row = jnp.sum(d_denom * query.astype(f32), axis=0, keepdims=True)
            put_state(wire, place, dot(d_numer.astype(bf16), query, 0, 0), row)


def inside_backward_kernel(
    core, queries, query_feat, key_feat, values, low, d_numer_in, d_denom_in, attn, gain, stats,
    kept, got, extra, extra_got, normed, query_grad, key_part, value_part,
    normed_slots, query_slots, sems,
):
    tokens, width = queries.shape
    copies = []
    heads_side = width // HEAD_DIM // CORES
    adds = core[0] == 1
    mask = causal(tokens)
    scale, _ = token_scales(stats[...], HEADS * HEAD_DIM)
    for wire, more, side in ((kept, extra, core[0]), (got, extra_got, 1 - core[0])):
        for place in range(heads_side):
            here = head_columns(side, place, heads_side)
            wide = pl.ds(pl.multiple_of((side * heads_side + place) * tokens, tokens), tokens)
            state, row = get_state(wire, more, adds, place)
            state_high, state_low = split(state)
            slot = len(copies) // 2
            normed_slots[slot] = (gain[:, here] * attn[:, here] * scale).astype(bf16)
            copies.append(send_out(normed_slots, normed, slot, here, sems.at[0, slot]))
            d_numer = d_numer_in[:, here]
            d_denom = d_denom_in[:, here]
            numer_low, numer_rest = split(d_numer)
            query = query_feat[:, here]
            key = key_feat[:, here]
            value = values[:, here]
            mixed = dot(numer_low, value, 1, 1) + jnp.concatenate([d_denom, d_denom], axis=1)
            mixed_low = jnp.where(mask, mixed, 0.0).astype(bf16)
            left = jnp.concatenate([numer_low, numer_low, numer_rest], axis=1)
            right = jnp.concatenate([state_high, state_low, state_high], axis=0)
            grad = dot(left, right, 1, 0) + d_denom * row + dot(mixed_low, key, 1, 0)
            query_raw = queries[:, here].astype(f32)
            query_slots[slot] = (grad * feature_slope(query_raw)).astype(bf16)
            copies.append(send_out(query_slots, query_grad, slot, here, sems.at[1, slot]))
            key_part[:, here] = dot(mixed_low, query, 0, 0)
            value_part[:, here] = dot(low[:, wide], numer_low, 0, 0)
    for copy in copies:
        copy.wait()


def outside_backward_kernel(
    core, keys, key_feat, values, key_part, value_part, kept, got, extra, extra_got,
    key_grad, value_grad, key_slots, value_slots, sems,
):
    width = keys.shape[1]
    copies = []
    heads_side = width // HEAD_DIM // CORES
    adds = core[0] == 0
    for wire, more, side in ((kept, extra, core[0]), (got, extra_got, 1 - core[0])):
        for place in range(heads_side):
            here = head_columns(side, place, heads_side)
            state, row = get_state(wire, more, adds, place)
            high, low = split(state)
            value = values[:, here]
            key = key_feat[:, here]
            grad = dot(
                jnp.concatenate([value, value], axis=1), jnp.concatenate([high, low], axis=0), 1, 0
            )
            grad = grad + row + key_part[:, here]
            key_raw = keys[:, here].astype(f32)
            slot = len(copies) // 2
            key_slots[slot] = (grad * feature_slope(key_raw)).astype(bf16)
            copies.append(send_out(key_slots, key_grad, slot, here, sems.at[0, slot]))
            grad = dot(
                jnp.concatenate([key, key], axis=1), jnp.concatenate([high, low], axis=1), 1, 1
            )
            value_slots[slot] = (grad + value_part[:, here]).astype(bf16)
            copies.append(send_out(value_slots, value_grad, slot, here, sems.at[1, slot]))
    for copy in copies:
        copy.wait()


def chip_sums_kernel(backward, spread, sums):
    chips = spread.shape[0]
    total = jnp.zeros(spread.shape[1:], f32)
    for step in range(chips):
        chip = chips - 1 - step if backward else step
        sums[chip] = total
        if step < chips - 1:
            total = total + spread[chip]


def shaped(shape, dtype):
    return jax.ShapeDtypeStruct(shape, dtype)


def call(kernel, name, out_shape, *operands, core=None, flops=0, hbm_in=(), hbm_out=(), slots=0):
    moved = sum(x.size * x.dtype.itemsize for x in operands)
    moved += sum(x.size * x.dtype.itemsize for x in jax.tree.leaves(out_shape))

    def spaces(count, hbm):
        kinds = [pltpu.HBM if place in hbm else pltpu.VMEM for place in range(count)]
        return [pl.BlockSpec(memory_space=kind) for kind in kinds]

    in_specs = spaces(len(operands), hbm_in)
    out_specs = spaces(len(jax.tree.leaves(out_shape)), hbm_out)
    scratch = []
    if slots:
        scratch = [pltpu.VMEM((slots, BLOCK, HEAD_DIM), bf16)] * 2
        scratch.append(pltpu.SemaphoreType.DMA((2, slots)))
    if core is not None:
        in_specs = [pl.BlockSpec(memory_space=pltpu.SMEM)] + in_specs
        operands = (core,) + operands
    return pl.pallas_call(
        kernel,
        out_shape=out_shape,
        in_specs=in_specs,
        out_specs=tuple(out_specs) if isinstance(out_shape, tuple) else out_specs[0],
        scratch_shapes=scratch,
        compiler_params=pltpu.CompilerParams(vmem_limit_bytes=16 << 20),
        cost_estimate=pl.CostEstimate(flops=flops, bytes_accessed=moved, transcendentals=0),
        name=name,
    )(*operands)


def swap_cores(array):
    return lax.ppermute(array, "core", [(0, 1), (1, 0)])


def chip_sums(spread, backward):
    kernel = functools.partial(chip_sums_kernel, backward)
    return call(kernel, "chip_sums", shaped(spread.shape, f32), spread)


def body(queries, key_rows, value_rows, norm_gain, out_grad):
    tokens, width = queries.shape
    heads = width // HEAD_DIM
    chips = lax.axis_size("chip")
    core = lax.axis_index("core").astype(jnp.int32).reshape(1)
    gain = norm_gain.reshape(1, width)
    wire = shaped((chips, ROWS + 1, HEAD_DIM), f32)
    narrow = shaped((tokens, width), bf16)
    full = shaped((tokens, width), f32)
    unit = 2 * tokens * HEAD_DIM * HEAD_DIM * heads

    mine, theirs = call(
        states_kernel,
        "states",
        (wire, wire),
        key_rows,
        value_rows,
        core=core,
        flops=unit,
        hbm_in=(0, 1),
        slots=heads,
    )
    theirs, mine, q_in, k_in, v_in = lax.optimization_barrier(
        (theirs, mine, queries, key_rows, value_rows)
    )
    extra = swap_cores(theirs)
    extra_got = swap_cores(mine)
    inside = call(
        inside_forward_kernel,
        "inside_forward",
        (narrow, narrow, shaped((tokens, heads * tokens), bf16), full, full),
        q_in,
        k_in,
        v_in,
        flops=4 * unit,
    )
    extra, extra_got, mine, inside = lax.optimization_barrier((extra, extra_got, mine, inside))
    query_feat, key_feat, low, numer_in, denom_in = inside
    spread = lax.all_to_all(mine + extra, "chip", 0, 0)
    kept = lax.all_to_all(chip_sums(spread, False), "chip", 0, 0)
    got = swap_cores(kept)
    prefix = (kept, got, extra, extra_got)
    attn, inverse, stats = call(
        attention_kernel,
        "attention",
        (full, full, shaped((8, tokens), f32)),
        query_feat,
        numer_in,
        denom_in,
        *prefix,
        gain,
        out_grad,
        core=core,
        flops=4 * unit,
    )
    stats = lax.psum(stats, "head")
    d_numer, d_denom, mine, theirs = call(
        gradient_kernel,
        "gradient",
        (full, full, wire, wire),
        query_feat,
        attn,
        inverse,
        gain,
        out_grad,
        stats,
        core=core,
        flops=unit,
    )
    theirs, mine, d_numer, d_denom = lax.optimization_barrier((theirs, mine, d_numer, d_denom))
    extra = swap_cores(theirs)
    extra_got = swap_cores(mine)
    inside = call(
        inside_backward_kernel,
        "inside_backward",
        (narrow, narrow, full, full),
        queries,
        query_feat,
        key_feat,
        value_rows,
        low,
        d_numer,
        d_denom,
        attn,
        gain,
        stats,
        *prefix,
        core=core,
        flops=11 * unit,
        hbm_out=(0, 1),
        slots=heads,
    )
    extra, extra_got, mine, inside = lax.optimization_barrier((extra, extra_got, mine, inside))
    normed, query_grad, key_part, value_part = inside
    spread = lax.all_to_all(mine + extra, "chip", 0, 0)
    kept = lax.all_to_all(chip_sums(spread, True), "chip", 0, 0)
    got = swap_cores(kept)
    key_grad, value_grad = call(
        outside_backward_kernel,
        "outside_backward",
        (narrow, narrow),
        key_rows,
        key_feat,
        value_rows,
        key_part,
        value_part,
        kept,
        got,
        extra,
        extra_got,
        core=core,
        flops=4 * unit,
        hbm_out=(0, 1),
        slots=heads,
    )
    return (normed, query_grad, key_grad, value_grad)


def solution(mesh):
    devices = mesh.devices
    fine = Mesh(
        devices.reshape(devices.shape[0] // CORES, CORES, devices.shape[1]),
        ("chip", "core", "head"),
    )
    rows = P(("chip", "core"), "head")
    return jax.shard_map(
        body,
        mesh=fine,
        in_specs=(rows, rows, rows, P("head"), rows),
        out_specs=(rows, rows, rows, rows),
        check_vma=False,
    )
```

```python
import functools

import jax
import jax.numpy as jnp
from jax import lax
from jax.experimental import pallas as pl
from jax.experimental.pallas import tpu as pltpu
from jax.sharding import Mesh
from jax.sharding import PartitionSpec as P

HEADS = 32
HEAD_DIM = 128
CORES = 2
SIDE = 4
ROWS = 64
BLOCK = 256
BLOCKS = HEAD_DIM // ROWS

f32 = jnp.float32
bf16 = jnp.bfloat16
highest = lax.Precision.HIGHEST


def feature(values):
    return jnp.where(values > 0, values + 1.0, jnp.exp(jnp.minimum(values, 0.0)))


def feature_slope(values):
    return jnp.where(values > 0, jnp.ones_like(values), jnp.exp(jnp.minimum(values, 0.0)))


def dot(left, right, left_dim, right_dim, precision=None):
    return lax.dot_general(
        left,
        right,
        (((left_dim,), (right_dim,)), ((), ())),
        precision=precision,
        preferred_element_type=f32,
    )


def split(values):
    high = values.astype(bf16)
    return high, (values - high.astype(f32)).astype(bf16)


def head_columns(side, place, heads_side):
    return pl.ds(pl.multiple_of((side * heads_side + place) * HEAD_DIM, HEAD_DIM), HEAD_DIM)


def put_state(wire, place, state, row):
    first = place * BLOCKS
    wire[first : first + BLOCKS, 0:ROWS, :] = state.reshape(BLOCKS, ROWS, HEAD_DIM)
    wire[first : first + 1, ROWS : ROWS + 1, :] = row.reshape(1, 1, HEAD_DIM)


def clear_rows(wire):
    wire[:, ROWS : ROWS + 1, :] = jnp.zeros((wire.shape[0], 1, HEAD_DIM), f32)


def get_state(wire, extra, adds, place):
    first = place * BLOCKS
    blocks = pl.ds(first, BLOCKS)
    state = wire[blocks, 0:ROWS, :] + jnp.where(adds, extra[blocks, 0:ROWS, :], 0.0)
    row = wire[first, ROWS : ROWS + 1, :] + jnp.where(adds, extra[first, ROWS : ROWS + 1, :], 0.0)
    return state.reshape(HEAD_DIM, HEAD_DIM), row


def send_out(slots, target, slot, here, sem):
    copy = pltpu.make_async_copy(slots.at[slot], target.at[:, here], sem)
    copy.start()
    return copy


def causal(tokens):
    rows = lax.broadcasted_iota(jnp.int32, (tokens, tokens), 0)
    cols = lax.broadcasted_iota(jnp.int32, (tokens, tokens), 1)
    return rows >= cols


def head_order(core, heads_side):
    return [(side, place) for side in (1 - core, core) for place in range(heads_side)]


def states_kernel(core, keys, values, mine, theirs, key_slots, value_slots, sems):
    heads_side = keys.shape[1] // HEAD_DIM // CORES
    order = head_order(core[0], heads_side)
    copies = []
    for slot, (side, place) in enumerate(order):
        here = head_columns(side, place, heads_side)
        pair = (
            pltpu.make_async_copy(keys.at[:, here], key_slots.at[slot], sems.at[0, slot]),
            pltpu.make_async_copy(values.at[:, here], value_slots.at[slot], sems.at[1, slot]),
        )
        for copy in pair:
            copy.start()
        copies.append(pair)
    clear_rows(theirs)
    clear_rows(mine)
    for slot, (side, place) in enumerate(order):
        for copy in copies[slot]:
            copy.wait()
        key_feat = feature(key_slots[slot].astype(f32)).astype(bf16)
        row = jnp.sum(key_feat.astype(f32), axis=0, keepdims=True)
        wire = theirs if slot < heads_side else mine
        put_state(wire, place, dot(value_slots[slot], key_feat, 0, 0), row)


def inside_forward_kernel(queries, keys, values, query_out, key_out, low_out, numer, denom):
    tokens, width = queries.shape
    mask = causal(tokens)
    for head in range(width // HEAD_DIM):
        here = pl.ds(head * HEAD_DIM, HEAD_DIM)
        query_feat = feature(queries[:, here].astype(f32)).astype(bf16)
        key_feat = feature(keys[:, here].astype(f32)).astype(bf16)
        query_out[:, here] = query_feat
        key_out[:, here] = key_feat
        scores = jnp.where(mask, dot(query_feat, key_feat, 1, 1), 0.0)
        scores_low = scores.astype(bf16)
        low_out[:, pl.ds(head * tokens, tokens)] = scores_low
        numer[:, here] = dot(scores_low, values[:, here], 1, 0)
        total = jnp.sum(scores, axis=1, keepdims=True)
        denom[:, here] = jnp.broadcast_to(total, (tokens, HEAD_DIM))


def attention_kernel(
    core, query_feat, numer_in, denom_in, kept, got, extra, extra_got, gain, out_grad,
    attn_out, inverse_out, stats,
):
    tokens, width = query_feat.shape
    heads_side = width // HEAD_DIM // CORES
    adds = core[0] == 1
    squares = jnp.zeros((tokens, HEAD_DIM), f32)
    cross = jnp.zeros((tokens, HEAD_DIM), f32)
    for wire, more, side in ((kept, extra, core[0]), (got, extra_got, 1 - core[0])):
        for place in range(heads_side):
            here = head_columns(side, place, heads_side)
            state, row = get_state(wire, more, adds, place)
            both = jnp.concatenate([state, jnp.broadcast_to(row, state.shape)], axis=0)
            right = jnp.concatenate(split(both), axis=1)
            query = query_feat[:, here]
            product = dot(jnp.concatenate([query, query], axis=1), right, 1, 1)
            numer = numer_in[:, here] + product[:, :HEAD_DIM]
            inverse = 1.0 / (denom_in[:, here] + product[:, HEAD_DIM:])
            attn = numer * inverse
            grad_in = gain[:, here] * out_grad[:, here].astype(f32)
            squares = squares + attn * attn
            cross = cross + attn * grad_in
            attn_out[:, here] = attn
            inverse_out[:, here] = inverse
    ones = jnp.ones((8, HEAD_DIM), f32)
    which = lax.broadcasted_iota(jnp.int32, (8, tokens), 0)
    row_squares = dot(ones, squares, 1, 1, highest)
    row_cross = dot(ones, cross, 1, 1, highest)
    stats[...] = jnp.where(which == 0, row_squares, jnp.where(which == 1, row_cross, 0.0))


def token_scales(stats, width_all):
    tokens = stats.shape[1]
    squares = stats[0:1, :]
    cross = stats[1:2, :]
    scale = lax.rsqrt(squares / width_all + 1e-06)
    slope = scale * scale * scale * (cross / width_all)
    which = lax.broadcasted_iota(jnp.int32, (8, tokens), 0)
    rows = jnp.where(which == 0, scale, jnp.where(which == 1, slope, 0.0))
    pick = lax.broadcasted_iota(jnp.int32, (8, 2 * HEAD_DIM), 0) == (
        lax.broadcasted_iota(jnp.int32, (8, 2 * HEAD_DIM), 1) // HEAD_DIM
    )
    spread = dot(rows, pick.astype(f32), 0, 0, highest)
    return spread[:, :HEAD_DIM], spread[:, HEAD_DIM:]


def gradient_kernel(
    core, query_feat, attn_in, inverse_in, gain, out_grad, stats, stats_a, stats_b, stats_c,
    numer_out, denom_out, mine, theirs, stats_out,
):
    width = query_feat.shape[1]
    heads_side = width // HEAD_DIM // CORES
    total = (stats[...] + stats_a[...]) + (stats_b[...] + stats_c[...])
    stats_out[...] = total
    scale, slope = token_scales(total, HEADS * HEAD_DIM)
    for wire, side in ((theirs, 1 - core[0]), (mine, core[0])):
        clear_rows(wire)
        for place in range(heads_side):
            here = head_columns(side, place, heads_side)
            attn = attn_in[:, here]
            inverse = inverse_in[:, here]
            grad_in = gain[:, here] * out_grad[:, here].astype(f32)
            d_attn = scale * grad_in - attn * slope
            d_numer = d_attn * inverse
            total = jnp.sum(d_attn * attn, axis=1, keepdims=True)
            d_denom = -total * inverse
            numer_out[:, here] = d_numer
            denom_out[:, here] = d_denom
            query = query_feat[:, here]
            row = jnp.sum(d_denom * query.astype(f32), axis=0, keepdims=True)
            put_state(wire, place, dot(d_numer.astype(bf16), query, 0, 0), row)


def inside_backward_kernel(
    core, queries, query_feat, key_feat, values, low, d_numer_in, d_denom_in, attn, gain, stats,
    kept, got, extra, extra_got, normed, query_grad, key_part, value_part,
    normed_slots, query_slots, sems,
):
    tokens, width = queries.shape
    copies = []
    heads_side = width // HEAD_DIM // CORES
    adds = core[0] == 1
    mask = causal(tokens)
    scale, _ = token_scales(stats[...], HEADS * HEAD_DIM)
    for wire, more, side in ((kept, extra, core[0]), (got, extra_got, 1 - core[0])):
        for place in range(heads_side):
            here = head_columns(side, place, heads_side)
            wide = pl.ds(pl.multiple_of((side * heads_side + place) * tokens, tokens), tokens)
            state, row = get_state(wire, more, adds, place)
            state_high, state_low = split(state)
            slot = len(copies) // 2
            normed_slots[slot] = (gain[:, here] * attn[:, here] * scale).astype(bf16)
            copies.append(send_out(normed_slots, normed, slot, here, sems.at[0, slot]))
            d_numer = d_numer_in[:, here]
            d_denom = d_denom_in[:, here]
            numer_low, numer_rest = split(d_numer)
            query = query_feat[:, here]
            key = key_feat[:, here]
            value = values[:, here]
            mixed = dot(numer_low, value, 1, 1) + jnp.concatenate([d_denom, d_denom], axis=1)
            mixed_low = jnp.where(mask, mixed, 0.0).astype(bf16)
            left = jnp.concatenate([numer_low, numer_low, numer_rest], axis=1)
            right = jnp.concatenate([state_high, state_low, state_high], axis=0)
            grad = dot(left, right, 1, 0) + d_denom * row + dot(mixed_low, key, 1, 0)
            query_raw = queries[:, here].astype(f32)
            query_slots[slot] = (grad * feature_slope(query_raw)).astype(bf16)
            copies.append(send_out(query_slots, query_grad, slot, here, sems.at[1, slot]))
            key_part[:, here] = dot(mixed_low, query, 0, 0)
            value_part[:, here] = dot(low[:, wide], numer_low, 0, 0)
    for copy in copies:
        copy.wait()


def outside_backward_kernel(
    core, keys, key_feat, values, key_part, value_part, kept, got, extra, extra_got,
    key_grad, value_grad, key_slots, value_slots, sems,
):
    width = keys.shape[1]
    copies = []
    heads_side = width // HEAD_DIM // CORES
    adds = core[0] == 0
    for wire, more, side in ((kept, extra, core[0]), (got, extra_got, 1 - core[0])):
        for place in range(heads_side):
            here = head_columns(side, place, heads_side)
            state, row = get_state(wire, more, adds, place)
            high, low = split(state)
            value = values[:, here]
            key = key_feat[:, here]
            grad = dot(
                jnp.concatenate([value, value], axis=1), jnp.concatenate([high, low], axis=0), 1, 0
            )
            grad = grad + row + key_part[:, here]
            key_raw = keys[:, here].astype(f32)
            slot = len(copies) // 2
            key_slots[slot] = (grad * feature_slope(key_raw)).astype(bf16)
            copies.append(send_out(key_slots, key_grad, slot, here, sems.at[0, slot]))
            grad = dot(
                jnp.concatenate([key, key], axis=1), jnp.concatenate([high, low], axis=1), 1, 1
            )
            value_slots[slot] = (grad + value_part[:, here]).astype(bf16)
            copies.append(send_out(value_slots, value_grad, slot, here, sems.at[1, slot]))
    for copy in copies:
        copy.wait()


def row_total_kernel(spread, total):
    value = spread[0]
    for chip in range(1, spread.shape[0]):
        value = value + spread[chip]
    total[...] = value


def chip_sums_kernel(backward, row, spread, *rest):
    *others, sums = rest
    chips = spread.shape[0]
    total = jnp.zeros(spread.shape[1:], f32)
    for step, other in enumerate(others, 1):
        inside = row[0] + step < SIDE if backward else row[0] >= step
        total = total + jnp.where(inside, other[...], 0.0)
    for step in range(chips):
        chip = chips - 1 - step if backward else step
        sums[chip] = total
        if step < chips - 1:
            total = total + spread[chip]


def shaped(shape, dtype):
    return jax.ShapeDtypeStruct(shape, dtype)


def call(kernel, name, out_shape, *operands, core=None, flops=0, hbm_in=(), hbm_out=(), slots=0):
    moved = sum(x.size * x.dtype.itemsize for x in operands)
    moved += sum(x.size * x.dtype.itemsize for x in jax.tree.leaves(out_shape))

    def spaces(count, hbm):
        kinds = [pltpu.HBM if place in hbm else pltpu.VMEM for place in range(count)]
        return [pl.BlockSpec(memory_space=kind) for kind in kinds]

    in_specs = spaces(len(operands), hbm_in)
    out_specs = spaces(len(jax.tree.leaves(out_shape)), hbm_out)
    scratch = []
    if slots:
        scratch = [pltpu.VMEM((slots, BLOCK, HEAD_DIM), bf16)] * 2
        scratch.append(pltpu.SemaphoreType.DMA((2, slots)))
    if core is not None:
        in_specs = [pl.BlockSpec(memory_space=pltpu.SMEM)] + in_specs
        operands = (core,) + operands
    return pl.pallas_call(
        kernel,
        out_shape=out_shape,
        in_specs=in_specs,
        out_specs=tuple(out_specs) if isinstance(out_shape, tuple) else out_specs[0],
        scratch_shapes=scratch,
        compiler_params=pltpu.CompilerParams(vmem_limit_bytes=16 << 20),
        cost_estimate=pl.CostEstimate(flops=flops, bytes_accessed=moved, transcendentals=0),
        name=name,
    )(*operands)


def swap_cores(array):
    return lax.ppermute(array, "core", [(0, 1), (1, 0)])


def shifted(array, axis, step):
    size = lax.axis_size(axis)
    return lax.ppermute(array, axis, [(i, (i + step) % size) for i in range(size)])


def scan_chips(pair, row, backward, inside):
    spread = lax.all_to_all(pair, "z", 0, 0)
    total = call(row_total_kernel, "row_total", shaped(spread.shape[1:], f32), spread)
    sign = -1 if backward else 1
    others = [shifted(total, "x", sign * step) for step in range(1, SIDE)]
    total, done = lax.optimization_barrier((total, inside[1:]))
    done = inside[0](*done)
    others, spread, done = lax.optimization_barrier((others, spread, done))
    kernel = functools.partial(chip_sums_kernel, backward)
    sums = call(kernel, "chip_sums", shaped(spread.shape, f32), spread, *others, core=row)
    return lax.all_to_all(sums, "z", 0, 0), done


def body(queries, key_rows, value_rows, norm_gain, out_grad):
    tokens, width = queries.shape
    heads = width // HEAD_DIM
    core = lax.axis_index("core").astype(jnp.int32).reshape(1)
    row = lax.axis_index("x").astype(jnp.int32).reshape(1)
    gain = norm_gain.reshape(1, width)
    wire = shaped((lax.axis_size("z"), ROWS + 1, HEAD_DIM), f32)
    narrow = shaped((tokens, width), bf16)
    full = shaped((tokens, width), f32)
    unit = 2 * tokens * HEAD_DIM * HEAD_DIM * heads

    mine, theirs = call(
        states_kernel,
        "states",
        (wire, wire),
        key_rows,
        value_rows,
        core=core,
        flops=unit,
        hbm_in=(0, 1),
        slots=heads,
    )
    extra = swap_cores(theirs)
    extra_got = swap_cores(mine)
    extra, extra_got, mine = lax.optimization_barrier((extra, extra_got, mine))

    def inside_forward(*operands):
        return call(
            inside_forward_kernel,
            "inside_forward",
            (narrow, narrow, shaped((tokens, heads * tokens), bf16), full, full),
            *operands,
            flops=4 * unit,
        )

    kept, inside = scan_chips(
        mine + extra, row, False, (inside_forward, queries, key_rows, value_rows)
    )
    query_feat, key_feat, low, numer_in, denom_in = inside
    got = swap_cores(kept)
    prefix = (kept, got, extra, extra_got)
    attn, inverse, stats = call(
        attention_kernel,
        "attention",
        (full, full, shaped((8, tokens), f32)),
        query_feat,
        numer_in,
        denom_in,
        *prefix,
        gain,
        out_grad,
        core=core,
        flops=4 * unit,
    )
    stats_from = [shifted(stats, "head", step) for step in (2, 1, 3)]
    d_numer, d_denom, mine, theirs, stats = call(
        gradient_kernel,
        "gradient",
        (full, full, wire, wire, shaped((8, tokens), f32)),
        query_feat,
        attn,
        inverse,
        gain,
        out_grad,
        stats,
        *stats_from,
        core=core,
        flops=unit,
    )
    extra = swap_cores(theirs)
    extra_got = swap_cores(mine)
    extra, extra_got, mine = lax.optimization_barrier((extra, extra_got, mine))

    def inside_backward(*operands):
        return call(
            inside_backward_kernel,
            "inside_backward",
            (narrow, narrow, full, full),
            *operands,
            core=core,
            flops=11 * unit,
            hbm_out=(0, 1),
            slots=heads,
        )

    operands = (queries, query_feat, key_feat, value_rows, low, d_numer, d_denom, attn, gain, stats)
    kept, inside = scan_chips(mine + extra, row, True, (inside_backward,) + operands + prefix)
    normed, query_grad, key_part, value_part = inside
    got = swap_cores(kept)
    key_grad, value_grad = call(
        outside_backward_kernel,
        "outside_backward",
        (narrow, narrow),
        key_rows,
        key_feat,
        value_rows,
        key_part,
        value_part,
        kept,
        got,
        extra,
        extra_got,
        core=core,
        flops=4 * unit,
        hbm_out=(0, 1),
        slots=heads,
    )
    return (normed, query_grad, key_grad, value_grad)


def solution(mesh):
    devices = mesh.devices
    fine = Mesh(
        devices.reshape(SIDE, devices.shape[0] // (SIDE * CORES), CORES, devices.shape[1]),
        ("x", "z", "core", "head"),
    )
    rows = P(("x", "z", "core"), "head")
    return jax.shard_map(
        body,
        mesh=fine,
        in_specs=(rows, rows, rows, P("head"), rows),
        out_specs=(rows, rows, rows, rows),
        check_vma=False,
    )
```

```python
import functools

import jax
import jax.numpy as jnp
from jax import lax
from jax.experimental import pallas as pl
from jax.experimental.pallas import tpu as pltpu
from jax.sharding import Mesh
from jax.sharding import PartitionSpec as P

HEADS = 32
HEAD_DIM = 128
CORES = 2
TOP = 2
ROWS = 32
BLOCK = 256
BLOCKS = HEAD_DIM // ROWS

f32 = jnp.float32
bf16 = jnp.bfloat16


def feature(values):
    return jnp.where(values > 0, values + 1.0, jnp.exp(jnp.minimum(values, 0.0)))


def feature_slope(values):
    return jnp.where(values > 0, jnp.ones_like(values), jnp.exp(jnp.minimum(values, 0.0)))


def dot(left, right, left_dim, right_dim):
    return lax.dot_general(
        left,
        right,
        (((left_dim,), (right_dim,)), ((), ())),
        preferred_element_type=f32,
    )


def split(values):
    high = values.astype(bf16)
    return high, (values - high.astype(f32)).astype(bf16)


def side_of(core, own):
    return core[0] if own else 1 - core[0]


def parts_of(values, axis):
    high, rest = split(values)
    middle = values - high.astype(f32)
    low = (middle - rest.astype(f32)).astype(bf16)
    return jnp.concatenate([high, rest, low], axis=axis)


def head_columns(side, place, heads_side):
    return pl.ds(pl.multiple_of((side * heads_side + place) * HEAD_DIM, HEAD_DIM), HEAD_DIM)


def columns(place, size=HEAD_DIM):
    return pl.ds(place * size, size)


def put_state(wire, place, state, row):
    first = place * BLOCKS
    wire[first : first + BLOCKS, 0:ROWS, :] = state.reshape(BLOCKS, ROWS, HEAD_DIM)
    wire[first : first + 1, ROWS : ROWS + 1, :] = row.reshape(1, 1, HEAD_DIM)


def clear_rows(wire):
    wire[:, ROWS : ROWS + 1, :] = jnp.zeros((wire.shape[0], 1, HEAD_DIM), f32)


def get_state(wire, extra, adds, place):
    first = place * BLOCKS
    blocks = pl.ds(first, BLOCKS)
    state = wire[blocks, 0:ROWS, :] + jnp.where(adds, extra[blocks, 0:ROWS, :], 0.0)
    row = wire[first, ROWS : ROWS + 1, :] + jnp.where(adds, extra[first, ROWS : ROWS + 1, :], 0.0)
    return state.reshape(HEAD_DIM, HEAD_DIM), row


def send_out(slots, target, slot, here, sem):
    copy = pltpu.make_async_copy(slots.at[slot], target.at[:, here], sem)
    copy.start()
    return copy


def causal(tokens):
    rows = lax.broadcasted_iota(jnp.int32, (tokens, tokens), 0)
    cols = lax.broadcasted_iota(jnp.int32, (tokens, tokens), 1)
    return rows >= cols


def key_features_kernel(core, keys, key_own, key_other):
    heads_side = keys.shape[1] // HEAD_DIM // CORES
    for target, own in ((key_other, False), (key_own, True)):
        for place in range(heads_side):
            here = head_columns(side_of(core, own), place, heads_side)
            target[:, columns(place)] = feature(keys[:, here].astype(f32)).astype(bf16)


def states_kernel(own, core, key_feat, values, wire):
    heads_side = key_feat.shape[1] // HEAD_DIM
    clear_rows(wire)
    for place in range(heads_side):
        here = head_columns(side_of(core, own), place, heads_side)
        key = key_feat[:, columns(place)]
        row = jnp.sum(key.astype(f32), axis=0, keepdims=True)
        put_state(wire, place, dot(values[:, here], key, 0, 0), row)


def inside_forward_kernel(own, core, queries, values, key_feat, query_out, low_out, numer, denom):
    tokens = queries.shape[0]
    heads_side = key_feat.shape[1] // HEAD_DIM
    mask = causal(tokens)
    for place in range(heads_side):
        here = head_columns(side_of(core, own), place, heads_side)
        there = columns(place)
        query_feat = feature(queries[:, here].astype(f32)).astype(bf16)
        query_out[:, there] = query_feat
        scores = jnp.where(mask, dot(query_feat, key_feat[:, there], 1, 1), 0.0)
        scores_low = scores.astype(bf16)
        low_out[:, columns(place, tokens)] = scores_low
        numer[:, there] = dot(scores_low, values[:, here], 1, 0)
        total = jnp.sum(scores, axis=1, keepdims=True)
        denom[:, there] = jnp.broadcast_to(total, (tokens, HEAD_DIM))


def attention_kernel(own, core, query_feat, numer_in, denom_in, wire, extra, gain, out_grad, *rest):
    tokens, width = query_feat.shape
    heads_side = width // HEAD_DIM
    adds = core[0] == 1
    if own:
        attn_out, inverse_out, squares_out, cross_out = rest
        squares = jnp.zeros((tokens, HEAD_DIM), f32)
        cross = jnp.zeros((tokens, HEAD_DIM), f32)
    else:
        squares_in, cross_in, attn_out, inverse_out, stats = rest
        squares = squares_in[...]
        cross = cross_in[...]
    for place in range(heads_side):
        here = head_columns(side_of(core, own), place, heads_side)
        there = columns(place)
        state, row = get_state(wire, extra, adds, place)
        both = jnp.concatenate([state, jnp.broadcast_to(row, state.shape)], axis=0)
        right = jnp.concatenate(split(both), axis=1)
        query = query_feat[:, there]
        product = dot(jnp.concatenate([query, query], axis=1), right, 1, 1)
        numer = numer_in[:, there] + product[:, :HEAD_DIM]
        inverse = 1.0 / (denom_in[:, there] + product[:, HEAD_DIM:])
        attn = numer * inverse
        grad_in = gain[:, here] * out_grad[:, here].astype(f32)
        squares = squares + attn * attn
        cross = cross + attn * grad_in
        attn_out[:, there] = attn
        inverse_out[:, there] = inverse
    if own:
        squares_out[...] = squares
        cross_out[...] = cross
    else:
        ones = jnp.ones((8, 3 * HEAD_DIM), bf16)
        which = lax.broadcasted_iota(jnp.int32, (8, tokens), 0)
        row_squares = dot(ones, parts_of(squares, 1), 1, 1)
        row_cross = dot(ones, parts_of(cross, 1), 1, 1)
        stats[...] = jnp.where(which == 0, row_squares, jnp.where(which == 1, row_cross, 0.0))


def token_scales(stats, width_all):
    tokens = stats.shape[1]
    squares = stats[0:1, :]
    cross = stats[1:2, :]
    scale = lax.rsqrt(squares / width_all + 1e-06)
    slope = scale * scale * scale * (cross / width_all)
    which = lax.broadcasted_iota(jnp.int32, (8, tokens), 0)
    rows = jnp.where(which == 0, scale, jnp.where(which == 1, slope, 0.0))
    pick = lax.broadcasted_iota(jnp.int32, (24, 2 * HEAD_DIM), 0) % 8 == (
        lax.broadcasted_iota(jnp.int32, (24, 2 * HEAD_DIM), 1) // HEAD_DIM
    )
    spread = dot(parts_of(rows, 0), pick.astype(f32).astype(bf16), 0, 0)
    return spread[:, :HEAD_DIM], spread[:, HEAD_DIM:]


def gradient_kernel(own, core, query_feat, attn_in, inverse_in, gain, out_grad, *rest):
    width = query_feat.shape[1]
    heads_side = width // HEAD_DIM
    if own:
        scale_in, slope_in, numer_out, denom_out, wire = rest
        scale = scale_in[...]
        slope = slope_in[...]
    else:
        parts, (numer_out, denom_out, wire, scale_out, slope_out) = rest[:-5], rest[-5:]
        total = (parts[0][...] + parts[1][...]) + (parts[2][...] + parts[3][...])
        scale, slope = token_scales(total, HEADS * HEAD_DIM)
        scale_out[...] = scale
        slope_out[...] = slope
    clear_rows(wire)
    for place in range(heads_side):
        here = head_columns(side_of(core, own), place, heads_side)
        there = columns(place)
        attn = attn_in[:, there]
        inverse = inverse_in[:, there]
        grad_in = gain[:, here] * out_grad[:, here].astype(f32)
        d_attn = scale * grad_in - attn * slope
        d_numer = d_attn * inverse
        total = jnp.sum(d_attn * attn, axis=1, keepdims=True)
        d_denom = -total * inverse
        numer_out[:, there] = d_numer
        denom_out[:, there] = d_denom
        query = query_feat[:, there]
        row = jnp.sum(d_denom * query.astype(f32), axis=0, keepdims=True)
        put_state(wire, place, dot(d_numer.astype(bf16), query, 0, 0), row)


def early_backward_kernel(core, gain, scale_in, *refs):
    halves, normed, parts = (refs[:3], refs[3:6]), refs[6], refs[7:9]
    normed_slots, _, sems = refs[9:]
    tokens, width_side = refs[0].shape
    heads_side = width_side // HEAD_DIM
    scale = scale_in[...]
    copies = []
    for half, own in enumerate((True, False)):
        attn, low, d_numer_in = halves[half]
        for place in range(heads_side):
            here = head_columns(side_of(core, own), place, heads_side)
            there = columns(place)
            slot = half * heads_side + place
            normed_slots[slot] = (gain[:, here] * attn[:, there] * scale).astype(bf16)
            copies.append(send_out(normed_slots, normed, slot, here, sems.at[0, slot]))
    for half in range(CORES):
        attn, low, d_numer_in = halves[half]
        for place in range(heads_side):
            there = columns(place)
            numer_low = d_numer_in[:, there].astype(bf16)
            parts[half][:, there] = dot(low[:, columns(place, tokens)], numer_low, 0, 0)
    for copy in copies:
        copy.wait()


def inside_backward_kernel(core, queries, values, *refs):
    halves, refs = (refs[:6], refs[6:12]), refs[12:]
    query_grad, parts, (query_slots, _, sems) = refs[0], refs[1:3], refs[3:]
    tokens, width = queries.shape
    heads_side = width // HEAD_DIM // CORES
    adds = core[0] == 1
    mask = causal(tokens)
    copies = []
    for half, own in enumerate((True, False)):
        query_feat, key_feat, d_numer_in, d_denom_in, wire, extra = halves[half]
        for place in range(heads_side):
            here = head_columns(side_of(core, own), place, heads_side)
            there = columns(place)
            slot = half * heads_side + place
            state, row = get_state(wire, extra, adds, place)
            state_high, state_low = split(state)
            d_denom = d_denom_in[:, there]
            numer_low, numer_rest = split(d_numer_in[:, there])
            key = key_feat[:, there]
            mixed = dot(numer_low, values[:, here], 1, 1)
            mixed = mixed + jnp.concatenate([d_denom, d_denom], axis=1)
            mixed_low = jnp.where(mask, mixed, 0.0).astype(bf16)
            left = jnp.concatenate([numer_low, numer_low, numer_rest], axis=1)
            right = jnp.concatenate([state_high, state_low, state_high], axis=0)
            grad = dot(left, right, 1, 0) + d_denom * row + dot(mixed_low, key, 1, 0)
            query_raw = queries[:, here].astype(f32)
            query_slots[slot] = (grad * feature_slope(query_raw)).astype(bf16)
            copies.append(send_out(query_slots, query_grad, slot, here, sems.at[0, slot]))
            parts[half][:, there] = dot(mixed_low, query_feat[:, there], 0, 0)
    for copy in copies:
        copy.wait()


def outside_backward_kernel(own, core, keys, values, key_feat, key_part, value_part, wire, extra, *rest):
    key_grad, value_grad, key_slots, value_slots, sems = rest[-5:]
    heads_side = key_feat.shape[1] // HEAD_DIM
    adds = core[0] == 0
    copies = []
    for place in range(heads_side):
        here = head_columns(side_of(core, own), place, heads_side)
        there = columns(place)
        state, row = get_state(wire, extra, adds, place)
        high, low = split(state)
        value = values[:, here]
        key = key_feat[:, there]
        grad = dot(
            jnp.concatenate([value, value], axis=1), jnp.concatenate([high, low], axis=0), 1, 0
        )
        grad = grad + row + key_part[:, there]
        key_raw = keys[:, here].astype(f32)
        key_slots[place] = (grad * feature_slope(key_raw)).astype(bf16)
        copies.append(send_out(key_slots, key_grad, place, here, sems.at[0, place]))
        grad = dot(
            jnp.concatenate([key, key], axis=1), jnp.concatenate([high, low], axis=1), 1, 1
        )
        value_slots[place] = (grad + value_part[:, there]).astype(bf16)
        copies.append(send_out(value_slots, value_grad, place, here, sems.at[1, place]))
    for copy in copies:
        copy.wait()


def group_total_kernel(spread, total):
    value = spread[0]
    for chip in range(1, spread.shape[0]):
        value = value + spread[chip]
    total[...] = value


def chip_sums_kernel(backward, top, spread, other, sums):
    chips = spread.shape[0]
    inside = top[0] == (0 if backward else TOP - 1)
    total = jnp.where(inside, other[...], 0.0)
    for step in range(chips):
        chip = chips - 1 - step if backward else step
        sums[chip] = total
        if step < chips - 1:
            total = total + spread[chip]


def shaped(shape, dtype):
    return jax.ShapeDtypeStruct(shape, dtype)


def call(
    kernel, name, out_shape, *operands, core=None, flops=0, hbm_in=(), hbm_out=(), slots=0,
    vmem=16, aliases=None,
):
    moved = sum(x.size * x.dtype.itemsize for x in operands)
    moved += sum(x.size * x.dtype.itemsize for x in jax.tree.leaves(out_shape))

    def spaces(count, hbm):
        kinds = [pltpu.HBM if place in hbm else pltpu.VMEM for place in range(count)]
        return [pl.BlockSpec(memory_space=kind) for kind in kinds]

    in_specs = spaces(len(operands), hbm_in)
    out_specs = spaces(len(jax.tree.leaves(out_shape)), hbm_out)
    scratch = []
    if slots:
        scratch = [pltpu.VMEM((slots, BLOCK, HEAD_DIM), bf16)] * 2
        scratch.append(pltpu.SemaphoreType.DMA((2, slots)))
    if core is not None:
        in_specs = [pl.BlockSpec(memory_space=pltpu.SMEM)] + in_specs
        operands = (core,) + operands
    return pl.pallas_call(
        kernel,
        out_shape=out_shape,
        in_specs=in_specs,
        out_specs=tuple(out_specs) if isinstance(out_shape, tuple) else out_specs[0],
        scratch_shapes=scratch,
        input_output_aliases=aliases or {},
        compiler_params=pltpu.CompilerParams(vmem_limit_bytes=vmem << 20),
        cost_estimate=pl.CostEstimate(flops=flops, bytes_accessed=moved, transcendentals=0),
        name=name,
    )(*operands)


def swap(array, axis):
    return lax.ppermute(array, axis, [(0, 1), (1, 0)])


def shifted(array, axis, step):
    size = lax.axis_size(axis)
    return lax.ppermute(array, axis, [(i, (i + step) % size) for i in range(size)])


def after(first, *later):
    return lax.optimization_barrier((first, later))


def scan_chips(pair, top, backward, inside=None, operands=()):
    spread = lax.all_to_all(pair, "chip", 0, 0)
    total = call(group_total_kernel, "group_total", shaped(spread.shape[1:], f32), spread)
    done = ()
    if inside is None:
        other = swap(total, "top")
    else:
        total, operands = after(total, *operands)
        other = swap(total, "top")
        done = inside(*operands)
    other, spread, done = lax.optimization_barrier((other, spread, done))
    kernel = functools.partial(chip_sums_kernel, backward)
    sums = call(kernel, "chip_sums", shaped(spread.shape, f32), spread, other, core=top)
    return lax.all_to_all(sums, "chip", 0, 0), done


def body(queries, key_rows, value_rows, norm_gain, out_grad):
    tokens, width = queries.shape
    heads = width // HEAD_DIM
    heads_side = heads // CORES
    core = lax.axis_index("core").astype(jnp.int32).reshape(1)
    top = lax.axis_index("top").astype(jnp.int32).reshape(1)
    core, top = lax.optimization_barrier((core, top))
    gain = norm_gain.reshape(1, width)
    wire = shaped((lax.axis_size("chip"), ROWS + 1, HEAD_DIM), f32)
    narrow = shaped((tokens, width), bf16)
    half_low = shaped((tokens, width // CORES), bf16)
    half = shaped((tokens, width // CORES), f32)
    square = shaped((tokens, heads_side * tokens), bf16)
    lanes = shaped((tokens, HEAD_DIM), f32)
    stats_shape = shaped((8, tokens), f32)
    unit = tokens * HEAD_DIM * HEAD_DIM * heads

    def side_call(kernel, name, own, *args, **named):
        kernel = functools.partial(kernel, own)
        return call(kernel, name + ("_own" if own else "_other"), *args, core=core, **named)

    key_own, key_other = call(
        key_features_kernel, "key_features", (half_low, half_low), key_rows, core=core
    )
    theirs = side_call(states_kernel, "states", False, wire, key_other, value_rows, flops=unit)
    theirs, (key_own,) = after(theirs, key_own)
    extra = swap(theirs, "core")
    mine = side_call(states_kernel, "states", True, wire, key_own, value_rows, flops=unit)
    mine, (key_own, queries_in) = after(mine, key_own, queries)
    extra_got = swap(mine, "core")
    halves = (half_low, square, half, half)
    inside = side_call(
        inside_forward_kernel, "inside_forward", True, halves, queries_in, value_rows, key_own,
        flops=4 * unit,
    )
    extra, extra_got, mine, inside = lax.optimization_barrier((extra, extra_got, mine, inside))
    query_own, low_own, numer, denom = inside
    kept, _ = scan_chips(mine + extra, top, False)
    kept, (queries_in, key_other) = after(kept, queries, key_other)
    got = swap(kept, "core")
    query_other, low_other, numer_other, denom_other = side_call(
        inside_forward_kernel, "inside_forward", False, halves, queries_in, value_rows, key_other,
        flops=4 * unit,
    )
    attn_own, inverse_own, squares, cross = side_call(
        attention_kernel, "attention", True, (half, half, lanes, lanes),
        query_own, numer, denom, kept, extra, gain, out_grad, flops=4 * unit,
    )
    attn_other, inverse_other, stats = side_call(
        attention_kernel, "attention", False, (half, half, stats_shape),
        query_other, numer_other, denom_other, got, extra_got, gain, out_grad, squares, cross,
        flops=4 * unit,
    )
    prefix_own = (kept, extra)
    prefix_other = (got, extra_got)
    stats_from = [shifted(stats, "head", step) for step in (2, 1, 3)]
    d_numer_other, d_denom_other, theirs, scale, slope = side_call(
        gradient_kernel, "gradient", False, (half, half, wire, lanes, lanes),
        query_other, attn_other, inverse_other, gain, out_grad, stats, *stats_from, flops=unit,
    )
    theirs, (scale, slope) = after(theirs, scale, slope)
    extra = swap(theirs, "core")
    d_numer_own, d_denom_own, mine = side_call(
        gradient_kernel, "gradient", True, (half, half, wire),
        query_own, attn_own, inverse_own, gain, out_grad, scale, slope, flops=unit,
    )

    mine, (scale,) = after(mine, scale)
    extra_got = swap(mine, "core")
    normed, value_part, value_part_other = call(
        early_backward_kernel, "early_backward", (narrow, half, half), gain, scale,
        attn_own, low_own, d_numer_own, attn_other, low_other, d_numer_other,
        core=core, flops=4 * unit, hbm_out=(0,), slots=heads,
    )
    extra, extra_got, mine, normed, value_part, value_part_other = lax.optimization_barrier(
        (extra, extra_got, mine, normed, value_part, value_part_other)
    )

    def inside_backward(*operands):
        return call(
            inside_backward_kernel, "inside_backward", (narrow, half, half),
            *operands, core=core, flops=18 * unit, hbm_out=(0,), slots=heads,
        )

    operands = (queries, value_rows)
    operands += (query_own, key_own, d_numer_own, d_denom_own) + prefix_own
    operands += (query_other, key_other, d_numer_other, d_denom_other) + prefix_other
    kept, inside = scan_chips(mine + extra, top, True, inside_backward, operands)
    query_grad, key_part, key_part_other = inside
    got = swap(kept, "core")
    last = dict(flops=4 * unit, hbm_out=(0, 1), slots=heads_side)
    key_grad, value_grad = side_call(
        outside_backward_kernel, "outside_backward", True, (narrow, narrow),
        key_rows, value_rows, key_own, key_part, value_part, kept, extra, **last,
    )
    key_grad, value_grad = side_call(
        outside_backward_kernel, "outside_backward", False, (narrow, narrow),
        key_rows, value_rows, key_other, key_part_other, value_part_other, got, extra_got,
        key_grad, value_grad, hbm_in=(7, 8), aliases={8: 0, 9: 1}, **last,
    )
    return (normed, query_grad, key_grad, value_grad)


def solution(mesh):
    devices = mesh.devices
    fine = Mesh(
        devices.reshape(TOP, devices.shape[0] // (TOP * CORES), CORES, devices.shape[1]),
        ("top", "chip", "core", "head"),
    )
    rows = P(("top", "chip", "core"), "head")
    return jax.shard_map(
        body,
        mesh=fine,
        in_specs=(rows, rows, rows, P("head"), rows),
        out_specs=(rows, rows, rows, rows),
        check_vma=False,
    )
```

```python
import functools

import jax
import jax.numpy as jnp
from jax import lax
from jax.experimental import pallas as pl
from jax.experimental.pallas import tpu as pltpu
from jax.sharding import Mesh
from jax.sharding import PartitionSpec as P

HEADS = 32
HEAD_DIM = 128
CORES = 2
TOP = 2
ROWS = 32
BLOCK = 256
BLOCKS = HEAD_DIM // ROWS

f32 = jnp.float32
bf16 = jnp.bfloat16


def feature(values):
    return jnp.where(values > 0, values + 1.0, jnp.exp(jnp.minimum(values, 0.0)))


def feature_slope(values):
    return jnp.where(values > 0, jnp.ones_like(values), jnp.exp(jnp.minimum(values, 0.0)))


def dot(left, right, left_dim, right_dim):
    return lax.dot_general(
        left,
        right,
        (((left_dim,), (right_dim,)), ((), ())),
        preferred_element_type=f32,
    )


def split(values):
    high = values.astype(bf16)
    return high, (values - high.astype(f32)).astype(bf16)


def side_of(core, own):
    return core[0] if own else 1 - core[0]


def parts_of(values, axis):
    high, rest = split(values)
    middle = values - high.astype(f32)
    low = (middle - rest.astype(f32)).astype(bf16)
    return jnp.concatenate([high, rest, low], axis=axis)


def head_columns(side, place, heads_side):
    return pl.ds(pl.multiple_of((side * heads_side + place) * HEAD_DIM, HEAD_DIM), HEAD_DIM)


def columns(place, size=HEAD_DIM):
    return pl.ds(place * size, size)


def put_state(wire, place, state, row):
    first = place * BLOCKS
    wire[first : first + BLOCKS, 0:ROWS, :] = state.reshape(BLOCKS, ROWS, HEAD_DIM)
    wire[first : first + 1, ROWS : ROWS + 1, :] = row.reshape(1, 1, HEAD_DIM)


def clear_rows(wire):
    wire[:, ROWS : ROWS + 1, :] = jnp.zeros((wire.shape[0], 1, HEAD_DIM), f32)


def get_state(wire, place):
    first = place * BLOCKS
    state = wire[first : first + BLOCKS, 0:ROWS, :]
    return state.reshape(HEAD_DIM, HEAD_DIM), wire[first, ROWS : ROWS + 1, :]


def send_out(slots, target, slot, here, sem):
    copy = pltpu.make_async_copy(slots.at[slot], target.at[:, here], sem)
    copy.start()
    return copy


def causal(tokens):
    rows = lax.broadcasted_iota(jnp.int32, (tokens, tokens), 0)
    cols = lax.broadcasted_iota(jnp.int32, (tokens, tokens), 1)
    return rows >= cols


def key_features_kernel(core, keys, key_own, key_other):
    heads_side = keys.shape[1] // HEAD_DIM // CORES
    for target, own in ((key_other, False), (key_own, True)):
        for place in range(heads_side):
            here = head_columns(side_of(core, own), place, heads_side)
            target[:, columns(place)] = feature(keys[:, here].astype(f32)).astype(bf16)


def states_kernel(own, core, key_feat, values, wire):
    heads_side = key_feat.shape[1] // HEAD_DIM
    clear_rows(wire)
    for place in range(heads_side):
        here = head_columns(side_of(core, own), place, heads_side)
        key = key_feat[:, columns(place)]
        row = jnp.sum(key.astype(f32), axis=0, keepdims=True)
        put_state(wire, place, dot(values[:, here], key, 0, 0), row)


def inside_forward_kernel(own, core, queries, values, key_feat, query_out, low_out, numer, denom):
    tokens = queries.shape[0]
    heads_side = key_feat.shape[1] // HEAD_DIM
    mask = causal(tokens)
    for place in range(heads_side):
        here = head_columns(side_of(core, own), place, heads_side)
        there = columns(place)
        query_feat = feature(queries[:, here].astype(f32)).astype(bf16)
        query_out[:, there] = query_feat
        scores = jnp.where(mask, dot(query_feat, key_feat[:, there], 1, 1), 0.0)
        scores_low = scores.astype(bf16)
        low_out[:, columns(place, tokens)] = scores_low
        numer[:, there] = dot(scores_low, values[:, here], 1, 0)
        total = jnp.sum(scores, axis=1, keepdims=True)
        denom[:, there] = jnp.broadcast_to(total, (tokens, HEAD_DIM))


def prepare_kernel(core, queries, keys, gain, out_grad, *outs):
    heads_side = queries.shape[1] // HEAD_DIM // CORES
    for half, own in enumerate((True, False)):
        grad_in, query_slope, key_slope = outs[3 * half : 3 * half + 3]
        for place in range(heads_side):
            here = head_columns(side_of(core, own), place, heads_side)
            there = columns(place)
            grad_in[:, there] = gain[:, here] * out_grad[:, here].astype(f32)
            query_slope[:, there] = feature_slope(queries[:, here].astype(f32))
            key_slope[:, there] = feature_slope(keys[:, here].astype(f32))


def attention_kernel(own, query_feat, numer_in, denom_in, wire, grad_in, *rest):
    tokens, width = query_feat.shape
    heads_side = width // HEAD_DIM
    if own:
        attn_out, inverse_out, squares_out, cross_out = rest
        squares = jnp.zeros((tokens, HEAD_DIM), f32)
        cross = jnp.zeros((tokens, HEAD_DIM), f32)
    else:
        squares_in, cross_in, attn_out, inverse_out, stats = rest
        squares = squares_in[...]
        cross = cross_in[...]
    for place in range(heads_side):
        there = columns(place)
        state, row = get_state(wire, place)
        both = jnp.concatenate([state, jnp.broadcast_to(row, state.shape)], axis=0)
        right = jnp.concatenate(split(both), axis=1)
        query = query_feat[:, there]
        product = dot(jnp.concatenate([query, query], axis=1), right, 1, 1)
        numer = numer_in[:, there] + product[:, :HEAD_DIM]
        inverse = 1.0 / (denom_in[:, there] + product[:, HEAD_DIM:])
        attn = numer * inverse
        squares = squares + attn * attn
        cross = cross + attn * grad_in[:, there]
        attn_out[:, there] = attn
        inverse_out[:, there] = inverse
    if own:
        squares_out[...] = squares
        cross_out[...] = cross
    else:
        ones = jnp.ones((8, 3 * HEAD_DIM), bf16)
        which = lax.broadcasted_iota(jnp.int32, (8, tokens), 0)
        row_squares = dot(ones, parts_of(squares, 1), 1, 1)
        row_cross = dot(ones, parts_of(cross, 1), 1, 1)
        stats[...] = jnp.where(which == 0, row_squares, jnp.where(which == 1, row_cross, 0.0))


def token_scales(stats, width_all):
    tokens = stats.shape[1]
    squares = stats[0:1, :]
    cross = stats[1:2, :]
    scale = lax.rsqrt(squares / width_all + 1e-06)
    slope = scale * scale * scale * (cross / width_all)
    which = lax.broadcasted_iota(jnp.int32, (8, tokens), 0)
    rows = jnp.where(which == 0, scale, jnp.where(which == 1, slope, 0.0))
    pick = lax.broadcasted_iota(jnp.int32, (24, 2 * HEAD_DIM), 0) % 8 == (
        lax.broadcasted_iota(jnp.int32, (24, 2 * HEAD_DIM), 1) // HEAD_DIM
    )
    spread = dot(parts_of(rows, 0), pick.astype(f32).astype(bf16), 0, 0)
    return spread[:, :HEAD_DIM], spread[:, HEAD_DIM:]


def gradient_kernel(own, query_feat, attn_in, inverse_in, grad_in, *rest):
    width = query_feat.shape[1]
    heads_side = width // HEAD_DIM
    if own:
        scale_in, slope_in, numer_out, denom_out, wire = rest
        scale = scale_in[...]
        slope = slope_in[...]
    else:
        parts, (numer_out, denom_out, wire, scale_out, slope_out) = rest[:-5], rest[-5:]
        total = (parts[0][...] + parts[1][...]) + (parts[2][...] + parts[3][...])
        scale, slope = token_scales(total, HEADS * HEAD_DIM)
        scale_out[...] = scale
        slope_out[...] = slope
    clear_rows(wire)
    for place in range(heads_side):
        there = columns(place)
        attn = attn_in[:, there]
        inverse = inverse_in[:, there]
        d_attn = scale * grad_in[:, there] - attn * slope
        d_numer = d_attn * inverse
        total = jnp.sum(d_attn * attn, axis=1, keepdims=True)
        d_denom = -total * inverse
        numer_out[:, there] = d_numer
        denom_out[:, there] = d_denom
        query = query_feat[:, there]
        row = jnp.sum(d_denom * query.astype(f32), axis=0, keepdims=True)
        put_state(wire, place, dot(d_numer.astype(bf16), query, 0, 0), row)


def early_backward_kernel(low_own, numer_own, low_other, numer_other, part_own, part_other):
    tokens = numer_own.shape[0]
    halves = ((low_own, numer_own, part_own), (low_other, numer_other, part_other))
    for low, d_numer, part in halves:
        for place in range(part.shape[1] // HEAD_DIM):
            there = columns(place)
            numer_low = d_numer[:, there].astype(bf16)
            part[:, there] = dot(low[:, columns(place, tokens)], numer_low, 0, 0)


def inside_backward_kernel(core, values, gain, scale_in, *refs):
    halves, refs = (refs[:7], refs[7:14]), refs[14:]
    normed, query_grad, part_own, part_other, normed_slots, query_slots, sems, mixed_slots = refs
    parts = (part_own, part_other)
    tokens, width = values.shape
    heads_side = width // HEAD_DIM // CORES
    mask = causal(tokens)
    scale = scale_in[...]
    copies = []
    for half, own in enumerate((True, False)):
        query_feat, key_feat, query_slope, d_numer_in, d_denom_in, attn, wire = halves[half]
        for place in range(heads_side):
            here = head_columns(side_of(core, own), place, heads_side)
            there = columns(place)
            slot = half * heads_side + place
            normed_slots[slot] = (gain[:, here] * attn[:, there] * scale).astype(bf16)
            copies.append(send_out(normed_slots, normed, slot, here, sems.at[0, slot]))
            state, row = get_state(wire, place)
            state_high, state_low = split(state)
            d_denom = d_denom_in[:, there]
            numer_low, numer_rest = split(d_numer_in[:, there])
            mixed = dot(numer_low, values[:, here], 1, 1)
            mixed = mixed + jnp.concatenate([d_denom, d_denom], axis=1)
            mixed_low = jnp.where(mask, mixed, 0.0).astype(bf16)
            mixed_slots[slot] = mixed_low
            left = jnp.concatenate([numer_low, numer_low, numer_rest], axis=1)
            right = jnp.concatenate([state_high, state_low, state_high], axis=0)
            grad = dot(left, right, 1, 0) + d_denom * row
            grad = grad + dot(mixed_low, key_feat[:, there], 1, 0)
            query_slots[slot] = (grad * query_slope[:, there]).astype(bf16)
            copies.append(send_out(query_slots, query_grad, slot, here, sems.at[1, slot]))
    for half in range(CORES):
        query_feat = halves[half][0]
        for place in range(heads_side):
            there = columns(place)
            mixed_low = mixed_slots[half * heads_side + place]
            parts[half][:, there] = dot(mixed_low, query_feat[:, there], 0, 0)
    for copy in copies:
        copy.wait()


def outside_backward_kernel(
    own, core, key_slope, values, key_feat, key_part, value_part, wire, *rest
):
    key_grad, value_grad, key_slots, value_slots, sems = rest[-5:]
    heads_side = key_feat.shape[1] // HEAD_DIM
    copies = []
    for place in range(heads_side):
        here = head_columns(side_of(core, own), place, heads_side)
        there = columns(place)
        state, row = get_state(wire, place)
        high, low = split(state)
        value = values[:, here]
        key = key_feat[:, there]
        grad = dot(
            jnp.concatenate([value, value], axis=1), jnp.concatenate([high, low], axis=0), 1, 0
        )
        grad = grad + row + key_part[:, there]
        key_slots[place] = (grad * key_slope[:, there]).astype(bf16)
        copies.append(send_out(key_slots, key_grad, place, here, sems.at[0, place]))
        grad = dot(
            jnp.concatenate([key, key], axis=1), jnp.concatenate([high, low], axis=1), 1, 1
        )
        value_slots[place] = (grad + value_part[:, there]).astype(bf16)
        copies.append(send_out(value_slots, value_grad, place, here, sems.at[1, place]))
    for copy in copies:
        copy.wait()


def group_total_kernel(spread, total):
    value = spread[0]
    for chip in range(1, spread.shape[0]):
        value = value + spread[chip]
    total[...] = value


def chip_sums_kernel(backward, top, spread, other, sums):
    chips = spread.shape[0]
    inside = top[0] == (0 if backward else TOP - 1)
    total = jnp.where(inside, other[...], 0.0)
    for step in range(chips):
        chip = chips - 1 - step if backward else step
        sums[chip] = total
        if step < chips - 1:
            total = total + spread[chip]


def halves_of(chips, top):
    size = chips // 2
    for half in range(2):
        yield pl.ds(half * size, size), pl.ds(lax.rem(half + top[0], 2) * size, size)


def pair_kernel(top, mine, extra, pair):
    for here, there in halves_of(pair.shape[0], top):
        pair[here] = mine[there] + extra[there]


def finish_kernel(backward, core, top, kept, mine, extra, own, send):
    later = core[0] == (0 if backward else 1)
    for here, there in halves_of(own.shape[0], top):
        own[here] = kept[there] + jnp.where(later, extra[here], 0.0)
        send[here] = kept[there] + jnp.where(later, 0.0, mine[here])


def shaped(shape, dtype):
    return jax.ShapeDtypeStruct(shape, dtype)


def call(
    kernel, name, out_shape, *operands, scalars=(), flops=0, hbm_in=(), hbm_out=(), slots=0,
    vmem=16, aliases=None, scratch=(),
):
    moved = sum(x.size * x.dtype.itemsize for x in operands)
    moved += sum(x.size * x.dtype.itemsize for x in jax.tree.leaves(out_shape))

    def spaces(count, hbm):
        kinds = [pltpu.HBM if place in hbm else pltpu.VMEM for place in range(count)]
        return [pl.BlockSpec(memory_space=kind) for kind in kinds]

    in_specs = spaces(len(operands), hbm_in)
    out_specs = spaces(len(jax.tree.leaves(out_shape)), hbm_out)
    scratch_shapes = []
    if slots:
        scratch_shapes = [pltpu.VMEM((slots, BLOCK, HEAD_DIM), bf16)] * 2
        scratch_shapes.append(pltpu.SemaphoreType.DMA((2, slots)))
    in_specs = [pl.BlockSpec(memory_space=pltpu.SMEM) for _ in scalars] + in_specs
    operands = scalars + operands
    return pl.pallas_call(
        kernel,
        out_shape=out_shape,
        in_specs=in_specs,
        out_specs=tuple(out_specs) if isinstance(out_shape, tuple) else out_specs[0],
        scratch_shapes=scratch_shapes + list(scratch),
        input_output_aliases=aliases or {},
        compiler_params=pltpu.CompilerParams(vmem_limit_bytes=vmem << 20),
        cost_estimate=pl.CostEstimate(flops=flops, bytes_accessed=moved, transcendentals=0),
        name=name,
    )(*operands)


def swap(array, axis):
    return lax.ppermute(array, axis, [(0, 1), (1, 0)])


def shifted(array, axis, step):
    size = lax.axis_size(axis)
    return lax.ppermute(array, axis, [(i, (i + step) % size) for i in range(size)])


def after(first, *later):
    return lax.optimization_barrier((first, later))


def scan_chips(mine, extra, core, top, backward, inside=None, operands=()):
    wire = shaped(mine.shape, f32)
    pair = call(pair_kernel, "pair", wire, mine, extra, scalars=(top,))
    spread = lax.all_to_all(pair, "chip", 0, 0)
    total = call(group_total_kernel, "group_total", shaped(spread.shape[1:], f32), spread)
    done = ()
    if inside is not None:
        total, operands = after(total, *operands)
    chips = spread.shape[0]
    facing = [(chip, chips + (chip + chips // 2) % chips) for chip in range(chips)]
    other = lax.ppermute(total, ("top", "chip"), facing + [(b, a) for a, b in facing])
    if inside is not None:
        done = inside(*operands)
    other, spread, done = lax.optimization_barrier((other, spread, done))
    kernel = functools.partial(chip_sums_kernel, backward)
    sums = call(kernel, "chip_sums", wire, spread, other, scalars=(top,))
    kept = lax.all_to_all(sums, "chip", 0, 0)
    kernel = functools.partial(finish_kernel, backward)
    own, send = call(kernel, "finish", (wire, wire), kept, mine, extra, scalars=(core, top))
    own, (send,) = after(own, send)
    return own, swap(send, "core"), done


def body(queries, key_rows, value_rows, norm_gain, out_grad):
    tokens, width = queries.shape
    heads = width // HEAD_DIM
    heads_side = heads // CORES
    core = lax.axis_index("core").astype(jnp.int32).reshape(1)
    top = lax.axis_index("top").astype(jnp.int32).reshape(1)
    core, top = lax.optimization_barrier((core, top))
    gain = norm_gain.reshape(1, width)
    wire = shaped((lax.axis_size("chip"), ROWS + 1, HEAD_DIM), f32)
    narrow = shaped((tokens, width), bf16)
    half_low = shaped((tokens, width // CORES), bf16)
    half = shaped((tokens, width // CORES), f32)
    square = shaped((tokens, heads_side * tokens), bf16)
    lanes = shaped((tokens, HEAD_DIM), f32)
    stats_shape = shaped((8, tokens), f32)
    unit = tokens * HEAD_DIM * HEAD_DIM * heads

    def side_call(kernel, name, own, *args, scalars=(core,), **named):
        kernel = functools.partial(kernel, own)
        return call(kernel, name + ("_own" if own else "_other"), *args, scalars=scalars, **named)

    key_own, key_other = call(
        key_features_kernel, "key_features", (half_low, half_low), key_rows, scalars=(core,)
    )
    theirs = side_call(states_kernel, "states", False, wire, key_other, value_rows, flops=unit)
    theirs, (key_own,) = after(theirs, key_own)
    extra = swap(theirs, "core")
    mine = side_call(states_kernel, "states", True, wire, key_own, value_rows, flops=unit)
    halves = (half_low, square, half, half)
    own_kernels = (queries, key_rows, value_rows, key_own, gain, out_grad)

    def inside_forward_own(queries, keys, values, key_own, gain, out_grad):
        first = side_call(
            inside_forward_kernel, "inside_forward", True, halves, queries, values, key_own,
            flops=4 * unit,
        )
        return first, call(
            prepare_kernel, "prepare", (half,) * 6, queries, keys, gain, out_grad,
            scalars=(core,), flops=unit,
        )

    kept, got, inside = scan_chips(
        mine, extra, core, top, False, inside_forward_own, own_kernels
    )
    (query_own, low_own, numer, denom), prepared = inside
    grad_own, query_slope, key_slope, grad_other, query_slope_other, key_slope_other = prepared
    kept, (key_other,) = after(kept, key_other)
    query_other, low_other, numer_other, denom_other = side_call(
        inside_forward_kernel, "inside_forward", False, halves, queries, value_rows, key_other,
        flops=4 * unit,
    )
    attn_own, inverse_own, squares, cross = side_call(
        attention_kernel, "attention", True, (half, half, lanes, lanes),
        query_own, numer, denom, kept, grad_own, flops=4 * unit, scalars=(),
    )
    attn_other, inverse_other, stats = side_call(
        attention_kernel, "attention", False, (half, half, stats_shape),
        query_other, numer_other, denom_other, got, grad_other, squares, cross,
        flops=4 * unit, scalars=(),
    )
    stats_from = [shifted(stats, "head", step) for step in (2, 1, 3)]
    d_numer_other, d_denom_other, theirs, scale, slope = side_call(
        gradient_kernel, "gradient", False, (half, half, wire, lanes, lanes),
        query_other, attn_other, inverse_other, grad_other, stats, *stats_from,
        flops=unit, scalars=(),
    )
    theirs, (scale, slope) = after(theirs, scale, slope)
    extra = swap(theirs, "core")
    d_numer_own, d_denom_own, mine = side_call(
        gradient_kernel, "gradient", True, (half, half, wire),
        query_own, attn_own, inverse_own, grad_own, scale, slope, flops=unit, scalars=(),
    )

    mine, (d_numer_own,) = after(mine, d_numer_own)
    value_part, value_part_other = call(
        early_backward_kernel, "early_backward", (half, half),
        low_own, d_numer_own, low_other, d_numer_other, flops=4 * unit,
    )
    extra, mine, value_part, value_part_other = lax.optimization_barrier(
        (extra, mine, value_part, value_part_other)
    )

    def inside_backward(*operands):
        return call(
            inside_backward_kernel, "inside_backward", (narrow, narrow, half, half),
            *operands, scalars=(core,), flops=18 * unit, hbm_out=(0, 1), slots=heads,
            scratch=(pltpu.VMEM((heads, tokens, tokens), bf16),),
        )

    operands = (value_rows, gain, scale)
    operands += (query_own, key_own, query_slope, d_numer_own, d_denom_own, attn_own, kept)
    operands += (query_other, key_other, query_slope_other, d_numer_other, d_denom_other)
    operands += (attn_other, got)
    kept, got, inside = scan_chips(mine, extra, core, top, True, inside_backward, operands)
    normed, query_grad, key_part, key_part_other = inside
    last = dict(flops=4 * unit, hbm_out=(0, 1), slots=heads_side)
    key_grad, value_grad = side_call(
        outside_backward_kernel, "outside_backward", True, (narrow, narrow),
        key_slope, value_rows, key_own, key_part, value_part, kept, **last,
    )
    key_grad, value_grad = side_call(
        outside_backward_kernel, "outside_backward", False, (narrow, narrow),
        key_slope_other, value_rows, key_other, key_part_other, value_part_other, got,
        key_grad, value_grad, hbm_in=(6, 7), aliases={7: 0, 8: 1}, **last,
    )
    return (normed, query_grad, key_grad, value_grad)


def solution(mesh):
    devices = mesh.devices
    fine = Mesh(
        devices.reshape(TOP, devices.shape[0] // (TOP * CORES), CORES, devices.shape[1]),
        ("top", "chip", "core", "head"),
    )
    rows = P(("top", "chip", "core"), "head")
    return jax.shard_map(
        body,
        mesh=fine,
        in_specs=(rows, rows, rows, P("head"), rows),
        out_specs=(rows, rows, rows, rows),
        check_vma=False,
    )
```

```python
import functools

import jax
import jax.numpy as jnp
from jax import lax
from jax.experimental import pallas as pl
from jax.experimental.pallas import tpu as pltpu
from jax.sharding import Mesh
from jax.sharding import PartitionSpec as P

HEADS = 32
HEAD_DIM = 128
CORES = 2
TOP = 2
ROWS = 32
BLOCK = 256
BLOCKS = HEAD_DIM // ROWS

f32 = jnp.float32
bf16 = jnp.bfloat16


def feature(values):
    return jnp.where(values > 0, values + 1.0, jnp.exp(jnp.minimum(values, 0.0)))


def feature_slope(values):
    return jnp.where(values > 0, jnp.ones_like(values), jnp.exp(jnp.minimum(values, 0.0)))


def dot(left, right, left_dim, right_dim):
    return lax.dot_general(
        left,
        right,
        (((left_dim,), (right_dim,)), ((), ())),
        preferred_element_type=f32,
    )


def split(values):
    high = values.astype(bf16)
    return high, (values - high.astype(f32)).astype(bf16)


def side_of(core, own):
    return core[0] if own else 1 - core[0]


def parts_of(values, axis):
    high, rest = split(values)
    middle = values - high.astype(f32)
    low = (middle - rest.astype(f32)).astype(bf16)
    return jnp.concatenate([high, rest, low], axis=axis)


def head_columns(side, place, heads_side):
    return pl.ds(pl.multiple_of((side * heads_side + place) * HEAD_DIM, HEAD_DIM), HEAD_DIM)


def columns(place, size=HEAD_DIM):
    return pl.ds(place * size, size)


def put_state(wire, place, state, row):
    first = place * BLOCKS
    wire[first : first + BLOCKS, 0:ROWS, :] = state.reshape(BLOCKS, ROWS, HEAD_DIM)
    wire[first : first + 1, ROWS : ROWS + 1, :] = row.reshape(1, 1, HEAD_DIM)


def clear_rows(wire):
    wire[:, ROWS : ROWS + 1, :] = jnp.zeros((wire.shape[0], 1, HEAD_DIM), f32)


def get_state(wire, place):
    first = place * BLOCKS
    state = wire[first : first + BLOCKS, 0:ROWS, :]
    return state.reshape(HEAD_DIM, HEAD_DIM), wire[first, ROWS : ROWS + 1, :]


def send_out(slots, target, slot, here, sem):
    copy = pltpu.make_async_copy(slots.at[slot], target.at[:, here], sem)
    copy.start()
    return copy


def causal(tokens):
    rows = lax.broadcasted_iota(jnp.int32, (tokens, tokens), 0)
    cols = lax.broadcasted_iota(jnp.int32, (tokens, tokens), 1)
    return rows >= cols


def key_features_kernel(core, keys, key_own, key_other):
    heads_side = keys.shape[1] // HEAD_DIM // CORES
    for target, own in ((key_other, False), (key_own, True)):
        for place in range(heads_side):
            here = head_columns(side_of(core, own), place, heads_side)
            target[:, columns(place)] = feature(keys[:, here].astype(f32)).astype(bf16)


def states_kernel(own, core, key_feat, values, wire):
    heads_side = key_feat.shape[1] // HEAD_DIM
    clear_rows(wire)
    for place in range(heads_side):
        here = head_columns(side_of(core, own), place, heads_side)
        key = key_feat[:, columns(place)]
        row = jnp.sum(key.astype(f32), axis=0, keepdims=True)
        put_state(wire, place, dot(values[:, here], key, 0, 0), row)


def inside_forward_kernel(own, core, queries, values, key_feat, query_out, low_out, numer, denom):
    tokens = queries.shape[0]
    heads_side = key_feat.shape[1] // HEAD_DIM
    mask = causal(tokens)
    for place in range(heads_side):
        here = head_columns(side_of(core, own), place, heads_side)
        there = columns(place)
        query_feat = feature(queries[:, here].astype(f32)).astype(bf16)
        query_out[:, there] = query_feat
        scores = jnp.where(mask, dot(query_feat, key_feat[:, there], 1, 1), 0.0)
        scores_low = scores.astype(bf16)
        low_out[:, columns(place, tokens)] = scores_low
        numer[:, there] = dot(scores_low, values[:, here], 1, 0)
        total = jnp.sum(scores, axis=1, keepdims=True)
        denom[:, there] = jnp.broadcast_to(total, (tokens, HEAD_DIM))


def prepare_kernel(core, queries, keys, gain, out_grad, *outs):
    heads_side = queries.shape[1] // HEAD_DIM // CORES
    for half, own in enumerate((True, False)):
        grad_in, query_slope, key_slope = outs[3 * half : 3 * half + 3]
        for place in range(heads_side):
            here = head_columns(side_of(core, own), place, heads_side)
            there = columns(place)
            grad_in[:, there] = gain[:, here] * out_grad[:, here].astype(f32)
            query_slope[:, there] = feature_slope(queries[:, here].astype(f32))
            key_slope[:, there] = feature_slope(keys[:, here].astype(f32))


def attention_kernel(own, query_feat, numer_in, denom_in, wire, grad_in, *rest):
    tokens, width = query_feat.shape
    heads_side = width // HEAD_DIM
    if own:
        attn_out, inverse_out, squares_out, cross_out = rest
        squares = jnp.zeros((tokens, HEAD_DIM), f32)
        cross = jnp.zeros((tokens, HEAD_DIM), f32)
    else:
        squares_in, cross_in, attn_out, inverse_out, stats = rest
        squares = squares_in[...]
        cross = cross_in[...]
    for place in range(heads_side):
        there = columns(place)
        state, row = get_state(wire, place)
        both = jnp.concatenate([state, jnp.broadcast_to(row, state.shape)], axis=0)
        right = jnp.concatenate(split(both), axis=1)
        query = query_feat[:, there]
        product = dot(jnp.concatenate([query, query], axis=1), right, 1, 1)
        numer = numer_in[:, there] + product[:, :HEAD_DIM]
        inverse = 1.0 / (denom_in[:, there] + product[:, HEAD_DIM:])
        attn = numer * inverse
        squares = squares + attn * attn
        cross = cross + attn * grad_in[:, there]
        attn_out[:, there] = attn
        inverse_out[:, there] = inverse
    if own:
        squares_out[...] = squares
        cross_out[...] = cross
    else:
        ones = jnp.ones((8, 3 * HEAD_DIM), bf16)
        which = lax.broadcasted_iota(jnp.int32, (8, tokens), 0)
        row_squares = dot(ones, parts_of(squares, 1), 1, 1)
        row_cross = dot(ones, parts_of(cross, 1), 1, 1)
        stats[...] = jnp.where(which == 0, row_squares, jnp.where(which == 1, row_cross, 0.0))


def token_scales(stats, width_all):
    tokens = stats.shape[1]
    squares = stats[0:1, :]
    cross = stats[1:2, :]
    scale = lax.rsqrt(squares / width_all + 1e-06)
    slope = scale * scale * scale * (cross / width_all)
    which = lax.broadcasted_iota(jnp.int32, (8, tokens), 0)
    rows = jnp.where(which == 0, scale, jnp.where(which == 1, slope, 0.0))
    pick = lax.broadcasted_iota(jnp.int32, (24, 2 * HEAD_DIM), 0) % 8 == (
        lax.broadcasted_iota(jnp.int32, (24, 2 * HEAD_DIM), 1) // HEAD_DIM
    )
    spread = dot(parts_of(rows, 0), pick.astype(f32).astype(bf16), 0, 0)
    return spread[:, :HEAD_DIM], spread[:, HEAD_DIM:]


def gradient_kernel(own, query_feat, attn_in, inverse_in, grad_in, *rest):
    width = query_feat.shape[1]
    heads_side = width // HEAD_DIM
    if own:
        scale_in, slope_in, numer_out, denom_out, wire = rest
        scale = scale_in[...]
        slope = slope_in[...]
    else:
        parts, (numer_out, denom_out, wire, scale_out, slope_out) = rest[:-5], rest[-5:]
        total = (parts[0][...] + parts[1][...]) + (parts[2][...] + parts[3][...])
        scale, slope = token_scales(total, HEADS * HEAD_DIM)
        scale_out[...] = scale
        slope_out[...] = slope
    clear_rows(wire)
    for place in range(heads_side):
        there = columns(place)
        attn = attn_in[:, there]
        inverse = inverse_in[:, there]
        d_attn = scale * grad_in[:, there] - attn * slope
        d_numer = d_attn * inverse
        total = jnp.sum(d_attn * attn, axis=1, keepdims=True)
        d_denom = -total * inverse
        numer_out[:, there] = d_numer
        denom_out[:, there] = d_denom
        query = query_feat[:, there]
        row = jnp.sum(d_denom * query.astype(f32), axis=0, keepdims=True)
        put_state(wire, place, dot(d_numer.astype(bf16), query, 0, 0), row)


def early_backward_kernel(low_own, numer_own, low_other, numer_other, part_own, part_other):
    tokens = numer_own.shape[0]
    halves = ((low_own, numer_own, part_own), (low_other, numer_other, part_other))
    for low, d_numer, part in halves:
        for place in range(part.shape[1] // HEAD_DIM):
            there = columns(place)
            numer_low = d_numer[:, there].astype(bf16)
            part[:, there] = dot(low[:, columns(place, tokens)], numer_low, 0, 0)


def inside_backward_kernel(core, values, gain, scale_in, *refs):
    halves, refs = (refs[:7], refs[7:14]), refs[14:]
    normed, query_grad, part_own, part_other, normed_slots, query_slots, sems, mixed_slots = refs
    parts = (part_own, part_other)
    tokens, width = values.shape
    heads_side = width // HEAD_DIM // CORES
    mask = causal(tokens)
    scale = scale_in[...]
    copies = []
    for half, own in enumerate((True, False)):
        query_feat, key_feat, query_slope, d_numer_in, d_denom_in, attn, wire = halves[half]
        for place in range(heads_side):
            here = head_columns(side_of(core, own), place, heads_side)
            there = columns(place)
            slot = half * heads_side + place
            normed_slots[slot] = (gain[:, here] * attn[:, there] * scale).astype(bf16)
            copies.append(send_out(normed_slots, normed, slot, here, sems.at[0, slot]))
            state, row = get_state(wire, place)
            state_high, state_low = split(state)
            d_denom = d_denom_in[:, there]
            numer_low, numer_rest = split(d_numer_in[:, there])
            mixed = dot(numer_low, values[:, here], 1, 1)
            mixed = mixed + jnp.concatenate([d_denom, d_denom], axis=1)
            mixed_low = jnp.where(mask, mixed, 0.0).astype(bf16)
            mixed_slots[slot] = mixed_low
            left = jnp.concatenate([numer_low, numer_low, numer_rest], axis=1)
            right = jnp.concatenate([state_high, state_low, state_high], axis=0)
            grad = dot(left, right, 1, 0) + d_denom * row
            grad = grad + dot(mixed_low, key_feat[:, there], 1, 0)
            query_slots[slot] = (grad * query_slope[:, there]).astype(bf16)
            copies.append(send_out(query_slots, query_grad, slot, here, sems.at[1, slot]))
    for half in range(CORES):
        query_feat = halves[half][0]
        for place in range(heads_side):
            there = columns(place)
            mixed_low = mixed_slots[half * heads_side + place]
            parts[half][:, there] = dot(mixed_low, query_feat[:, there], 0, 0)
    for copy in copies:
        copy.wait()


def outside_backward_kernel(
    own, core, key_slope, values, key_feat, key_part, value_part, wire, *rest
):
    key_grad, value_grad, key_slots, value_slots, sems = rest[-5:]
    heads_side = key_feat.shape[1] // HEAD_DIM
    copies = []
    for place in range(heads_side):
        here = head_columns(side_of(core, own), place, heads_side)
        there = columns(place)
        state, row = get_state(wire, place)
        high, low = split(state)
        value = values[:, here]
        key = key_feat[:, there]
        grad = dot(
            jnp.concatenate([value, value], axis=1), jnp.concatenate([high, low], axis=0), 1, 0
        )
        grad = grad + row + key_part[:, there]
        key_slots[place] = (grad * key_slope[:, there]).astype(bf16)
        copies.append(send_out(key_slots, key_grad, place, here, sems.at[0, place]))
        grad = dot(
            jnp.concatenate([key, key], axis=1), jnp.concatenate([high, low], axis=1), 1, 1
        )
        value_slots[place] = (grad + value_part[:, there]).astype(bf16)
        copies.append(send_out(value_slots, value_grad, place, here, sems.at[1, place]))
    for copy in copies:
        copy.wait()


def chunk(place):
    return pl.ds(place * (ROWS + 1), ROWS + 1)


def group_total_kernel(spread, total):
    value = spread[chunk(0), :]
    for chip in range(1, spread.shape[0] // (ROWS + 1)):
        value = value + spread[chunk(chip), :]
    total[...] = value


def chip_sums_kernel(backward, top, spread, other, sums):
    chips = spread.shape[0] // (ROWS + 1)
    inside = top[0] == (0 if backward else TOP - 1)
    total = jnp.where(inside, other[...], 0.0)
    for step in range(chips):
        chip = chips - 1 - step if backward else step
        sums[chunk(chip), :] = total
        if step < chips - 1:
            total = total + spread[chunk(chip), :]


def pair_kernel(top, mine, extra, pair):
    size = mine.shape[0] // 2
    for half in range(2):
        first = lax.rem(half + top[0], 2) * size
        for place in range(size):
            value = mine[first + place] + extra[first + place]
            pair[chunk(half * size + place), :] = value


def finish_kernel(backward, core, top, kept, mine, extra, own, send):
    size = mine.shape[0] // 2
    later = core[0] == (0 if backward else 1)
    for half in range(2):
        first = pl.multiple_of(lax.rem(half + top[0], 2) * (size * (ROWS + 1)), 8)
        block = kept[pl.ds(first, size * (ROWS + 1)), :]
        for place in range(size):
            here = half * size + place
            value = block[place * (ROWS + 1) : (place + 1) * (ROWS + 1)]
            own[here] = value + jnp.where(later, extra[here], 0.0)
            send[here] = value + jnp.where(later, 0.0, mine[here])


def shaped(shape, dtype):
    return jax.ShapeDtypeStruct(shape, dtype)


def call(
    kernel, name, out_shape, *operands, scalars=(), flops=0, hbm_in=(), hbm_out=(), slots=0,
    vmem=16, aliases=None, scratch=(),
):
    moved = sum(x.size * x.dtype.itemsize for x in operands)
    moved += sum(x.size * x.dtype.itemsize for x in jax.tree.leaves(out_shape))

    def spaces(count, hbm):
        kinds = [pltpu.HBM if place in hbm else pltpu.VMEM for place in range(count)]
        return [pl.BlockSpec(memory_space=kind) for kind in kinds]

    in_specs = spaces(len(operands), hbm_in)
    out_specs = spaces(len(jax.tree.leaves(out_shape)), hbm_out)
    scratch_shapes = []
    if slots:
        scratch_shapes = [pltpu.VMEM((slots, BLOCK, HEAD_DIM), bf16)] * 2
        scratch_shapes.append(pltpu.SemaphoreType.DMA((2, slots)))
    in_specs = [pl.BlockSpec(memory_space=pltpu.SMEM) for _ in scalars] + in_specs
    operands = scalars + operands
    return pl.pallas_call(
        kernel,
        out_shape=out_shape,
        in_specs=in_specs,
        out_specs=tuple(out_specs) if isinstance(out_shape, tuple) else out_specs[0],
        scratch_shapes=scratch_shapes + list(scratch),
        input_output_aliases=aliases or {},
        compiler_params=pltpu.CompilerParams(vmem_limit_bytes=vmem << 20),
        cost_estimate=pl.CostEstimate(flops=flops, bytes_accessed=moved, transcendentals=0),
        name=name,
    )(*operands)


def swap(array, axis):
    return lax.ppermute(array, axis, [(0, 1), (1, 0)])


def shifted(array, axis, step):
    size = lax.axis_size(axis)
    return lax.ppermute(array, axis, [(i, (i + step) % size) for i in range(size)])


def after(first, *later):
    return lax.optimization_barrier((first, later))


def exchange(flat, chips):
    chunks = flat.reshape(chips, 1, flat.size // chips)
    return lax.all_to_all(chunks, "chip", 0, 0).reshape(flat.shape)


def scan_chips(mine, extra, core, top, backward, inside=None, operands=()):
    wire = shaped(mine.shape, f32)
    chips, rows, lanes = mine.shape
    flat = shaped((chips * rows, lanes), f32)
    pair = call(pair_kernel, "pair", flat, mine, extra, scalars=(top,))
    spread = exchange(pair, chips)
    total = call(group_total_kernel, "group_total", shaped((rows, lanes), f32), spread)
    done = ()
    if inside is not None:
        total, operands = after(total, *operands)
    facing = [(chip, chips + (chip + chips // 2) % chips) for chip in range(chips)]
    other = lax.ppermute(total, ("top", "chip"), facing + [(b, a) for a, b in facing])
    if inside is not None:
        done = inside(*operands)
    other, spread, done = lax.optimization_barrier((other, spread, done))
    kernel = functools.partial(chip_sums_kernel, backward)
    sums = call(kernel, "chip_sums", flat, spread, other, scalars=(top,))
    kept = exchange(sums, chips)
    kernel = functools.partial(finish_kernel, backward)
    own, send = call(kernel, "finish", (wire, wire), kept, mine, extra, scalars=(core, top))
    own, (send,) = after(own, send)
    return own, swap(send, "core"), done


def body(queries, key_rows, value_rows, norm_gain, out_grad):
    tokens, width = queries.shape
    heads = width // HEAD_DIM
    heads_side = heads // CORES
    core = lax.axis_index("core").astype(jnp.int32).reshape(1)
    top = lax.axis_index("top").astype(jnp.int32).reshape(1)
    core, top = lax.optimization_barrier((core, top))
    gain = norm_gain.reshape(1, width)
    wire = shaped((lax.axis_size("chip"), ROWS + 1, HEAD_DIM), f32)
    narrow = shaped((tokens, width), bf16)
    half_low = shaped((tokens, width // CORES), bf16)
    half = shaped((tokens, width // CORES), f32)
    square = shaped((tokens, heads_side * tokens), bf16)
    lanes = shaped((tokens, HEAD_DIM), f32)
    stats_shape = shaped((8, tokens), f32)
    unit = tokens * HEAD_DIM * HEAD_DIM * heads

    def side_call(kernel, name, own, *args, scalars=(core,), **named):
        kernel = functools.partial(kernel, own)
        return call(kernel, name + ("_own" if own else "_other"), *args, scalars=scalars, **named)

    key_own, key_other = call(
        key_features_kernel, "key_features", (half_low, half_low), key_rows, scalars=(core,)
    )
    theirs = side_call(states_kernel, "states", False, wire, key_other, value_rows, flops=unit)
    theirs, (key_own,) = after(theirs, key_own)
    extra = swap(theirs, "core")
    mine = side_call(states_kernel, "states", True, wire, key_own, value_rows, flops=unit)
    halves = (half_low, square, half, half)
    own_kernels = (queries, key_rows, value_rows, key_own, gain, out_grad)

    def inside_forward_own(queries, keys, values, key_own, gain, out_grad):
        first = side_call(
            inside_forward_kernel, "inside_forward", True, halves, queries, values, key_own,
            flops=4 * unit,
        )
        return first, call(
            prepare_kernel, "prepare", (half,) * 6, queries, keys, gain, out_grad,
            scalars=(core,), flops=unit,
        )

    kept, got, inside = scan_chips(
        mine, extra, core, top, False, inside_forward_own, own_kernels
    )
    (query_own, low_own, numer, denom), prepared = inside
    grad_own, query_slope, key_slope, grad_other, query_slope_other, key_slope_other = prepared
    kept, (key_other,) = after(kept, key_other)
    query_other, low_other, numer_other, denom_other = side_call(
        inside_forward_kernel, "inside_forward", False, halves, queries, value_rows, key_other,
        flops=4 * unit,
    )
    attn_own, inverse_own, squares, cross = side_call(
        attention_kernel, "attention", True, (half, half, lanes, lanes),
        query_own, numer, denom, kept, grad_own, flops=4 * unit, scalars=(),
    )
    attn_other, inverse_other, stats = side_call(
        attention_kernel, "attention", False, (half, half, stats_shape),
        query_other, numer_other, denom_other, got, grad_other, squares, cross,
        flops=4 * unit, scalars=(),
    )
    stats_from = [shifted(stats, "head", step) for step in (2, 1, 3)]
    d_numer_other, d_denom_other, theirs, scale, slope = side_call(
        gradient_kernel, "gradient", False, (half, half, wire, lanes, lanes),
        query_other, attn_other, inverse_other, grad_other, stats, *stats_from,
        flops=unit, scalars=(),
    )
    theirs, (scale, slope) = after(theirs, scale, slope)
    extra = swap(theirs, "core")
    d_numer_own, d_denom_own, mine = side_call(
        gradient_kernel, "gradient", True, (half, half, wire),
        query_own, attn_own, inverse_own, grad_own, scale, slope, flops=unit, scalars=(),
    )

    mine, (d_numer_own,) = after(mine, d_numer_own)
    value_part, value_part_other = call(
        early_backward_kernel, "early_backward", (half, half),
        low_own, d_numer_own, low_other, d_numer_other, flops=4 * unit,
    )
    extra, mine, value_part, value_part_other = lax.optimization_barrier(
        (extra, mine, value_part, value_part_other)
    )

    def inside_backward(*operands):
        return call(
            inside_backward_kernel, "inside_backward", (narrow, narrow, half, half),
            *operands, scalars=(core,), flops=18 * unit, hbm_out=(0, 1), slots=heads,
            scratch=(pltpu.VMEM((heads, tokens, tokens), bf16),),
        )

    operands = (value_rows, gain, scale)
    operands += (query_own, key_own, query_slope, d_numer_own, d_denom_own, attn_own, kept)
    operands += (query_other, key_other, query_slope_other, d_numer_other, d_denom_other)
    operands += (attn_other, got)
    kept, got, inside = scan_chips(mine, extra, core, top, True, inside_backward, operands)
    normed, query_grad, key_part, key_part_other = inside
    last = dict(flops=4 * unit, hbm_out=(0, 1), slots=heads_side)
    key_grad, value_grad = side_call(
        outside_backward_kernel, "outside_backward", True, (narrow, narrow),
        key_slope, value_rows, key_own, key_part, value_part, kept, **last,
    )
    key_grad, value_grad = side_call(
        outside_backward_kernel, "outside_backward", False, (narrow, narrow),
        key_slope_other, value_rows, key_other, key_part_other, value_part_other, got,
        key_grad, value_grad, hbm_in=(6, 7), aliases={7: 0, 8: 1}, **last,
    )
    return (normed, query_grad, key_grad, value_grad)


def solution(mesh):
    devices = mesh.devices
    fine = Mesh(
        devices.reshape(TOP, devices.shape[0] // (TOP * CORES), CORES, devices.shape[1]),
        ("top", "chip", "core", "head"),
    )
    rows = P(("top", "chip", "core"), "head")
    return jax.shard_map(
        body,
        mesh=fine,
        in_specs=(rows, rows, rows, P("head"), rows),
        out_specs=(rows, rows, rows, rows),
        check_vma=False,
    )
```

```python
import functools

import jax
import jax.numpy as jnp
from jax import lax
from jax.experimental import pallas as pl
from jax.experimental.pallas import tpu as pltpu
from jax.sharding import Mesh
from jax.sharding import PartitionSpec as P

HEADS = 32
HEAD_DIM = 128
CORES = 2
TOP = 2
ROWS = 32
BLOCK = 256
BLOCKS = HEAD_DIM // ROWS

f32 = jnp.float32
bf16 = jnp.bfloat16


def feature(values):
    return jnp.where(values > 0, values + 1.0, jnp.exp(jnp.minimum(values, 0.0)))


def feature_slope(values):
    return jnp.where(values > 0, jnp.ones_like(values), jnp.exp(jnp.minimum(values, 0.0)))


def dot(left, right, left_dim, right_dim):
    return lax.dot_general(
        left,
        right,
        (((left_dim,), (right_dim,)), ((), ())),
        preferred_element_type=f32,
    )


def split(values):
    high = values.astype(bf16)
    return high, (values - high.astype(f32)).astype(bf16)


def side_of(core, own):
    return core[0] if own else 1 - core[0]


def parts_of(values, axis):
    high, rest = split(values)
    middle = values - high.astype(f32)
    low = (middle - rest.astype(f32)).astype(bf16)
    return jnp.concatenate([high, rest, low], axis=axis)


def head_columns(side, place, heads_side):
    return pl.ds(pl.multiple_of((side * heads_side + place) * HEAD_DIM, HEAD_DIM), HEAD_DIM)


def columns(place, size=HEAD_DIM):
    return pl.ds(place * size, size)


def chunk(place, first=0, size=ROWS + 1):
    return pl.ds(place * (ROWS + 1) + first, size)


def put_state(wire, place, state, row):
    for block in range(BLOCKS):
        here = place * BLOCKS + block
        wire[chunk(here, 0, ROWS), :] = state[block * ROWS : (block + 1) * ROWS]
        wire[chunk(here, ROWS, 1), :] = jnp.zeros_like(row) if block else row


def get_state(wire, place):
    blocks = [wire[chunk(place * BLOCKS + block, 0, ROWS), :] for block in range(BLOCKS)]
    return jnp.concatenate(blocks, axis=0), wire[chunk(place * BLOCKS, ROWS, 1), :]


def send_out(slots, target, slot, here, sem):
    copy = pltpu.make_async_copy(slots.at[slot], target.at[:, here], sem)
    copy.start()
    return copy


def causal(tokens):
    rows = lax.broadcasted_iota(jnp.int32, (tokens, tokens), 0)
    cols = lax.broadcasted_iota(jnp.int32, (tokens, tokens), 1)
    return rows >= cols


def key_features_kernel(core, keys, key_out):
    heads_side = key_out.shape[1] // HEAD_DIM
    for place in range(heads_side):
        here = head_columns(side_of(core, False), place, heads_side)
        key_out[:, columns(place)] = feature(keys[:, here].astype(f32)).astype(bf16)


def states_kernel(own, core, keys, values, wire, *key_out):
    heads_side = keys.shape[1] // HEAD_DIM // (CORES if own else 1)
    for place in range(heads_side):
        here = head_columns(side_of(core, own), place, heads_side)
        if own:
            key = feature(keys[:, here].astype(f32)).astype(bf16)
            key_out[0][:, columns(place)] = key
        else:
            key = keys[:, columns(place)]
        row = jnp.sum(key.astype(f32), axis=0, keepdims=True)
        put_state(wire, place, dot(values[:, here], key, 0, 0), row)


def inside_forward_kernel(own, core, queries, values, key_feat, query_out, low_out, numer, denom):
    tokens = queries.shape[0]
    heads_side = key_feat.shape[1] // HEAD_DIM
    mask = causal(tokens)
    for place in range(heads_side):
        here = head_columns(side_of(core, own), place, heads_side)
        there = columns(place)
        query_feat = feature(queries[:, here].astype(f32)).astype(bf16)
        query_out[:, there] = query_feat
        scores = jnp.where(mask, dot(query_feat, key_feat[:, there], 1, 1), 0.0)
        scores_low = scores.astype(bf16)
        low_out[:, columns(place, tokens)] = scores_low
        numer[:, there] = dot(scores_low, values[:, here], 1, 0)
        total = jnp.sum(scores, axis=1, keepdims=True)
        denom[:, there] = jnp.broadcast_to(total, (tokens, HEAD_DIM))


def prepare_kernel(core, queries, keys, gain, out_grad, *outs):
    heads_side = queries.shape[1] // HEAD_DIM // CORES
    for half, own in enumerate((True, False)):
        grad_in, query_slope, key_slope = outs[3 * half : 3 * half + 3]
        for place in range(heads_side):
            here = head_columns(side_of(core, own), place, heads_side)
            there = columns(place)
            grad_in[:, there] = gain[:, here] * out_grad[:, here].astype(f32)
            query_slope[:, there] = feature_slope(queries[:, here].astype(f32))
            key_slope[:, there] = feature_slope(keys[:, here].astype(f32))


def attention_kernel(own, query_feat, numer_in, denom_in, wire, grad_in, *rest):
    tokens, width = query_feat.shape
    heads_side = width // HEAD_DIM
    if own:
        attn_out, inverse_out, squares_out, cross_out = rest
        squares = jnp.zeros((tokens, HEAD_DIM), f32)
        cross = jnp.zeros((tokens, HEAD_DIM), f32)
    else:
        squares_in, cross_in, attn_out, inverse_out, stats = rest
        squares = squares_in[...]
        cross = cross_in[...]
    for place in range(heads_side):
        there = columns(place)
        state, row = get_state(wire, place)
        both = jnp.concatenate([state, jnp.broadcast_to(row, state.shape)], axis=0)
        right = jnp.concatenate(split(both), axis=1)
        query = query_feat[:, there]
        product = dot(jnp.concatenate([query, query], axis=1), right, 1, 1)
        numer = numer_in[:, there] + product[:, :HEAD_DIM]
        inverse = 1.0 / (denom_in[:, there] + product[:, HEAD_DIM:])
        attn = numer * inverse
        squares = squares + attn * attn
        cross = cross + attn * grad_in[:, there]
        attn_out[:, there] = attn
        inverse_out[:, there] = inverse
    if own:
        squares_out[...] = squares
        cross_out[...] = cross
    else:
        ones = jnp.ones((8, 3 * HEAD_DIM), bf16)
        which = lax.broadcasted_iota(jnp.int32, (8, tokens), 0)
        row_squares = dot(ones, parts_of(squares, 1), 1, 1)
        row_cross = dot(ones, parts_of(cross, 1), 1, 1)
        stats[...] = jnp.where(which == 0, row_squares, jnp.where(which == 1, row_cross, 0.0))


def token_scales(stats, width_all):
    tokens = stats.shape[1]
    squares = stats[0:1, :]
    cross = stats[1:2, :]
    scale = lax.rsqrt(squares / width_all + 1e-06)
    slope = scale * scale * scale * (cross / width_all)
    which = lax.broadcasted_iota(jnp.int32, (8, tokens), 0)
    rows = jnp.where(which == 0, scale, jnp.where(which == 1, slope, 0.0))
    pick = lax.broadcasted_iota(jnp.int32, (24, 2 * HEAD_DIM), 0) % 8 == (
        lax.broadcasted_iota(jnp.int32, (24, 2 * HEAD_DIM), 1) // HEAD_DIM
    )
    spread = dot(parts_of(rows, 0), pick.astype(f32).astype(bf16), 0, 0)
    return spread[:, :HEAD_DIM], spread[:, HEAD_DIM:]


def gradient_kernel(own, query_feat, attn_in, inverse_in, grad_in, *rest):
    width = query_feat.shape[1]
    heads_side = width // HEAD_DIM
    if own:
        scale_in, slope_in, numer_out, denom_out, wire = rest
        scale = scale_in[...]
        slope = slope_in[...]
    else:
        parts, (numer_out, denom_out, wire, scale_out, slope_out) = rest[:-5], rest[-5:]
        total = (parts[0][...] + parts[1][...]) + (parts[2][...] + parts[3][...])
        scale, slope = token_scales(total, HEADS * HEAD_DIM)
        scale_out[...] = scale
        slope_out[...] = slope
    for place in range(heads_side):
        there = columns(place)
        attn = attn_in[:, there]
        inverse = inverse_in[:, there]
        d_attn = scale * grad_in[:, there] - attn * slope
        d_numer = d_attn * inverse
        total = jnp.sum(d_attn * attn, axis=1, keepdims=True)
        d_denom = -total * inverse
        numer_out[:, there] = d_numer
        denom_out[:, there] = d_denom
        query = query_feat[:, there]
        row = jnp.sum(d_denom * query.astype(f32), axis=0, keepdims=True)
        put_state(wire, place, dot(d_numer.astype(bf16), query, 0, 0), row)


def early_backward_kernel(low_own, numer_own, low_other, numer_other, part_own, part_other):
    tokens = numer_own.shape[0]
    halves = ((low_own, numer_own, part_own), (low_other, numer_other, part_other))
    for low, d_numer, part in halves:
        for place in range(part.shape[1] // HEAD_DIM):
            there = columns(place)
            numer_low = d_numer[:, there].astype(bf16)
            part[:, there] = dot(low[:, columns(place, tokens)], numer_low, 0, 0)


def inside_backward_kernel(core, values, gain, scale_in, *refs):
    halves, refs = (refs[:7], refs[7:14]), refs[14:]
    normed, query_grad, part_own, part_other, normed_slots, query_slots, sems, mixed_slots = refs
    parts = (part_own, part_other)
    tokens, width = values.shape
    heads_side = width // HEAD_DIM // CORES
    mask = causal(tokens)
    scale = scale_in[...]
    copies = []
    for half, own in enumerate((True, False)):
        query_feat, key_feat, query_slope, d_numer_in, d_denom_in, attn, wire = halves[half]
        for place in range(heads_side):
            here = head_columns(side_of(core, own), place, heads_side)
            there = columns(place)
            slot = half * heads_side + place
            normed_slots[slot] = (gain[:, here] * attn[:, there] * scale).astype(bf16)
            copies.append(send_out(normed_slots, normed, slot, here, sems.at[0, slot]))
            state, row = get_state(wire, place)
            state_high, state_low = split(state)
            d_denom = d_denom_in[:, there]
            numer_low, numer_rest = split(d_numer_in[:, there])
            mixed = dot(numer_low, values[:, here], 1, 1)
            mixed = mixed + jnp.concatenate([d_denom, d_denom], axis=1)
            mixed_low = jnp.where(mask, mixed, 0.0).astype(bf16)
            mixed_slots[slot] = mixed_low
            left = jnp.concatenate([numer_low, numer_low, numer_rest], axis=1)
            right = jnp.concatenate([state_high, state_low, state_high], axis=0)
            grad = dot(left, right, 1, 0) + d_denom * row
            grad = grad + dot(mixed_low, key_feat[:, there], 1, 0)
            query_slots[slot] = (grad * query_slope[:, there]).astype(bf16)
            copies.append(send_out(query_slots, query_grad, slot, here, sems.at[1, slot]))
    for half in range(CORES):
        query_feat = halves[half][0]
        for place in range(heads_side):
            there = columns(place)
            mixed_low = mixed_slots[half * heads_side + place]
            parts[half][:, there] = dot(mixed_low, query_feat[:, there], 0, 0)
    for copy in copies:
        copy.wait()


def outside_backward_kernel(
    own, core, key_slope, values, key_feat, key_part, value_part, wire, *rest
):
    key_grad, value_grad, key_slots, value_slots, sems = rest[-5:]
    heads_side = key_feat.shape[1] // HEAD_DIM
    copies = []
    for place in range(heads_side):
        here = head_columns(side_of(core, own), place, heads_side)
        there = columns(place)
        state, row = get_state(wire, place)
        high, low = split(state)
        value = values[:, here]
        key = key_feat[:, there]
        grad = dot(
            jnp.concatenate([value, value], axis=1), jnp.concatenate([high, low], axis=0), 1, 0
        )
        grad = grad + row + key_part[:, there]
        key_slots[place] = (grad * key_slope[:, there]).astype(bf16)
        copies.append(send_out(key_slots, key_grad, place, here, sems.at[0, place]))
        grad = dot(
            jnp.concatenate([key, key], axis=1), jnp.concatenate([high, low], axis=1), 1, 1
        )
        value_slots[place] = (grad + value_part[:, there]).astype(bf16)
        copies.append(send_out(value_slots, value_grad, place, here, sems.at[1, place]))
    for copy in copies:
        copy.wait()


def group_total_kernel(spread, total):
    value = spread[chunk(0), :]
    for chip in range(1, spread.shape[0] // (ROWS + 1)):
        value = value + spread[chunk(chip), :]
    total[...] = value


def chip_sums_kernel(backward, top, spread, other, sums):
    chips = spread.shape[0] // (ROWS + 1)
    inside = top[0] == (0 if backward else TOP - 1)
    total = jnp.where(inside, other[...], 0.0)
    for step in range(chips):
        chip = chips - 1 - step if backward else step
        sums[chunk(chip), :] = total
        if step < chips - 1:
            total = total + spread[chunk(chip), :]


def halves_of(rows, top):
    size = rows // 2
    for half in range(2):
        there = pl.multiple_of(lax.rem(half + top[0], 2) * size, 8)
        yield pl.ds(half * size, size), pl.ds(there, size)


def pair_kernel(top, mine, extra, pair):
    for here, there in halves_of(pair.shape[0], top):
        pair[here, :] = mine[there, :] + extra[there, :]


def finish_kernel(backward, core, top, kept, mine, extra, own, send):
    later = core[0] == (0 if backward else 1)
    for here, there in halves_of(own.shape[0], top):
        own[here, :] = kept[there, :] + jnp.where(later, extra[here, :], 0.0)
        send[here, :] = kept[there, :] + jnp.where(later, 0.0, mine[here, :])


def shaped(shape, dtype):
    return jax.ShapeDtypeStruct(shape, dtype)


def call(
    kernel, name, out_shape, *operands, scalars=(), flops=0, hbm_in=(), hbm_out=(), slots=0,
    vmem=16, aliases=None, scratch=(),
):
    moved = sum(x.size * x.dtype.itemsize for x in operands)
    moved += sum(x.size * x.dtype.itemsize for x in jax.tree.leaves(out_shape))

    def spaces(count, hbm):
        kinds = [pltpu.HBM if place in hbm else pltpu.VMEM for place in range(count)]
        return [pl.BlockSpec(memory_space=kind) for kind in kinds]

    in_specs = spaces(len(operands), hbm_in)
    out_specs = spaces(len(jax.tree.leaves(out_shape)), hbm_out)
    scratch_shapes = []
    if slots:
        scratch_shapes = [pltpu.VMEM((slots, BLOCK, HEAD_DIM), bf16)] * 2
        scratch_shapes.append(pltpu.SemaphoreType.DMA((2, slots)))
    in_specs = [pl.BlockSpec(memory_space=pltpu.SMEM) for _ in scalars] + in_specs
    operands = scalars + operands
    return pl.pallas_call(
        kernel,
        out_shape=out_shape,
        in_specs=in_specs,
        out_specs=tuple(out_specs) if isinstance(out_shape, tuple) else out_specs[0],
        scratch_shapes=scratch_shapes + list(scratch),
        input_output_aliases=aliases or {},
        compiler_params=pltpu.CompilerParams(vmem_limit_bytes=vmem << 20),
        cost_estimate=pl.CostEstimate(flops=flops, bytes_accessed=moved, transcendentals=0),
        name=name,
    )(*operands)


def swap(array, axis):
    return lax.ppermute(array, axis, [(0, 1), (1, 0)])


def swap_pairs(array, axis, order):
    pairs = [(a, b) for a, b in zip(order[::2], order[1::2])]
    return lax.ppermute(array, axis, pairs + [(b, a) for a, b in pairs])


def after(first, *later):
    return lax.optimization_barrier((first, later))


def exchange(flat, chips):
    chunks = flat.reshape(chips, 1, flat.size // chips)
    return lax.all_to_all(chunks, "chip", 0, 0).reshape(flat.shape)


def scan_chips(mine, extra, core, top, backward, inside=None, operands=()):
    wire = shaped(mine.shape, f32)
    chips = lax.axis_size("chip")
    pair = call(pair_kernel, "pair", wire, mine, extra, scalars=(top,))
    spread = exchange(pair, chips)
    total = call(group_total_kernel, "group_total", shaped((ROWS + 1, HEAD_DIM), f32), spread)
    done = ()
    if inside is not None:
        total, operands = after(total, *operands)
    facing = [(chip, chips + (chip + chips // 2) % chips) for chip in range(chips)]
    other = lax.ppermute(total, ("top", "chip"), facing + [(b, a) for a, b in facing])
    if inside is not None:
        done = inside(*operands)
    other, spread, done = lax.optimization_barrier((other, spread, done))
    kernel = functools.partial(chip_sums_kernel, backward)
    sums = call(kernel, "chip_sums", wire, spread, other, scalars=(top,))
    kept = exchange(sums, chips)
    kernel = functools.partial(finish_kernel, backward)
    own, send = call(kernel, "finish", (wire, wire), kept, mine, extra, scalars=(core, top))
    own, (send,) = after(own, send)
    return own, swap(send, "core"), done


def body(queries, key_rows, value_rows, norm_gain, out_grad):
    tokens, width = queries.shape
    heads = width // HEAD_DIM
    heads_side = heads // CORES
    core = lax.axis_index("core").astype(jnp.int32).reshape(1)
    top = lax.axis_index("top").astype(jnp.int32).reshape(1)
    core, top = lax.optimization_barrier((core, top))
    gain = norm_gain.reshape(1, width)
    wire = shaped((lax.axis_size("chip") * (ROWS + 1), HEAD_DIM), f32)
    narrow = shaped((tokens, width), bf16)
    half_low = shaped((tokens, width // CORES), bf16)
    half = shaped((tokens, width // CORES), f32)
    square = shaped((tokens, heads_side * tokens), bf16)
    lanes = shaped((tokens, HEAD_DIM), f32)
    stats_shape = shaped((8, tokens), f32)
    unit = tokens * HEAD_DIM * HEAD_DIM * heads

    def side_call(kernel, name, own, *args, scalars=(core,), **named):
        kernel = functools.partial(kernel, own)
        return call(kernel, name + ("_own" if own else "_other"), *args, scalars=scalars, **named)

    key_other = call(
        key_features_kernel, "key_features", half_low, key_rows, scalars=(core,)
    )
    theirs = side_call(states_kernel, "states", False, wire, key_other, value_rows, flops=unit)
    theirs, (keys, values) = after(theirs, key_rows, value_rows)
    extra = swap(theirs, "core")
    mine, key_own = side_call(
        states_kernel, "states", True, (wire, half_low), keys, values, flops=unit
    )
    halves = (half_low, square, half, half)
    own_kernels = (queries, key_rows, value_rows, key_own, gain, out_grad)

    def inside_forward_own(queries, keys, values, key_own, gain, out_grad):
        first = side_call(
            inside_forward_kernel, "inside_forward", True, halves, queries, values, key_own,
            flops=4 * unit,
        )
        return first, call(
            prepare_kernel, "prepare", (half,) * 6, queries, keys, gain, out_grad,
            scalars=(core,), flops=unit,
        )

    kept, got, inside = scan_chips(
        mine, extra, core, top, False, inside_forward_own, own_kernels
    )
    (query_own, low_own, numer, denom), prepared = inside
    grad_own, query_slope, key_slope, grad_other, query_slope_other, key_slope_other = prepared
    kept, (key_other,) = after(kept, key_other)
    query_other, low_other, numer_other, denom_other = side_call(
        inside_forward_kernel, "inside_forward", False, halves, queries, value_rows, key_other,
        flops=4 * unit,
    )
    attn_own, inverse_own, squares, cross = side_call(
        attention_kernel, "attention", True, (half, half, lanes, lanes),
        query_own, numer, denom, kept, grad_own, flops=4 * unit, scalars=(),
    )
    attn_other, inverse_other, stats = side_call(
        attention_kernel, "attention", False, (half, half, stats_shape),
        query_other, numer_other, denom_other, got, grad_other, squares, cross,
        flops=4 * unit, scalars=(),
    )
    stats_from = [
        swap_pairs(stats, "head", order)
        for order in ((0, 1, 2, 3), (1, 2, 3, 0), (0, 2, 1, 3))
    ]
    d_numer_other, d_denom_other, theirs, scale, slope = side_call(
        gradient_kernel, "gradient", False, (half, half, wire, lanes, lanes),
        query_other, attn_other, inverse_other, grad_other, stats, *stats_from,
        flops=unit, scalars=(),
    )
    theirs, (scale, slope) = after(theirs, scale, slope)
    extra = swap(theirs, "core")
    d_numer_own, d_denom_own, mine = side_call(
        gradient_kernel, "gradient", True, (half, half, wire),
        query_own, attn_own, inverse_own, grad_own, scale, slope, flops=unit, scalars=(),
    )

    mine, (d_numer_own,) = after(mine, d_numer_own)
    value_part, value_part_other = call(
        early_backward_kernel, "early_backward", (half, half),
        low_own, d_numer_own, low_other, d_numer_other, flops=4 * unit,
    )
    extra, mine, value_part, value_part_other = lax.optimization_barrier(
        (extra, mine, value_part, value_part_other)
    )

    def inside_backward(*operands):
        return call(
            inside_backward_kernel, "inside_backward", (narrow, narrow, half, half),
            *operands, scalars=(core,), flops=18 * unit, hbm_out=(0, 1), slots=heads,
            scratch=(pltpu.VMEM((heads, tokens, tokens), bf16),),
        )

    operands = (value_rows, gain, scale)
    operands += (query_own, key_own, query_slope, d_numer_own, d_denom_own, attn_own, kept)
    operands += (query_other, key_other, query_slope_other, d_numer_other, d_denom_other)
    operands += (attn_other, got)
    kept, got, inside = scan_chips(mine, extra, core, top, True, inside_backward, operands)
    normed, query_grad, key_part, key_part_other = inside
    last = dict(flops=4 * unit, hbm_out=(0, 1), slots=heads_side)
    key_grad, value_grad = side_call(
        outside_backward_kernel, "outside_backward", True, (narrow, narrow),
        key_slope, value_rows, key_own, key_part, value_part, kept, **last,
    )
    key_grad, value_grad = side_call(
        outside_backward_kernel, "outside_backward", False, (narrow, narrow),
        key_slope_other, value_rows, key_other, key_part_other, value_part_other, got,
        key_grad, value_grad, hbm_in=(6, 7), aliases={7: 0, 8: 1}, **last,
    )
    return (normed, query_grad, key_grad, value_grad)


def solution(mesh):
    devices = mesh.devices
    fine = Mesh(
        devices.reshape(TOP, devices.shape[0] // (TOP * CORES), CORES, devices.shape[1]),
        ("top", "chip", "core", "head"),
    )
    rows = P(("top", "chip", "core"), "head")
    return jax.shard_map(
        body,
        mesh=fine,
        in_specs=(rows, rows, rows, P("head"), rows),
        out_specs=(rows, rows, rows, rows),
        check_vma=False,
    )
```

```python
import functools

import jax
import jax.numpy as jnp
from jax import lax
from jax.experimental import pallas as pl
from jax.experimental.pallas import tpu as pltpu
from jax.sharding import Mesh
from jax.sharding import PartitionSpec as P

HEADS = 32
HEAD_DIM = 128
CORES = 2
TOP = 2
ROWS = 32
BLOCK = 256
GANG = 2
BLOCKS = HEAD_DIM // ROWS

f32 = jnp.float32
bf16 = jnp.bfloat16


def feature(values):
    return jnp.where(values > 0, values + 1.0, jnp.exp(jnp.minimum(values, 0.0)))


def feature_slope(values):
    return jnp.where(values > 0, jnp.ones_like(values), jnp.exp(jnp.minimum(values, 0.0)))


def dot(left, right, left_dim, right_dim):
    return lax.dot_general(
        left,
        right,
        (((left_dim,), (right_dim,)), ((), ())),
        preferred_element_type=f32,
    )


def split(values):
    high = values.astype(bf16)
    return high, (values - high.astype(f32)).astype(bf16)


def side_of(core, own):
    return core[0] if own else 1 - core[0]


def parts_of(values, axis):
    high, rest = split(values)
    middle = values - high.astype(f32)
    low = (middle - rest.astype(f32)).astype(bf16)
    return jnp.concatenate([high, rest, low], axis=axis)


def head_columns(side, place, heads_side):
    return pl.ds(pl.multiple_of((side * heads_side + place) * HEAD_DIM, HEAD_DIM), HEAD_DIM)


def columns(place, size=HEAD_DIM):
    return pl.ds(place * size, size)


def chunk(place, first=0, size=ROWS + 1):
    return pl.ds(place * (ROWS + 1) + first, size)


def put_state(wire, place, state, row):
    for block in range(BLOCKS):
        here = place * BLOCKS + block
        wire[chunk(here, 0, ROWS), :] = state[block * ROWS : (block + 1) * ROWS]
        wire[chunk(here, ROWS, 1), :] = jnp.zeros_like(row) if block else row


def get_state(wire, place):
    blocks = [wire[chunk(place * BLOCKS + block, 0, ROWS), :] for block in range(BLOCKS)]
    return jnp.concatenate(blocks, axis=0), wire[chunk(place * BLOCKS, ROWS, 1), :]


def put_out(slots, target, sems, slot, side, heads_side, value):
    place = slot % GANG
    slots[slot // GANG, :, columns(place)] = value
    if place != GANG - 1:
        return []
    first = (side * heads_side + slot % heads_side - place) * HEAD_DIM
    here = pl.ds(pl.multiple_of(first, HEAD_DIM), GANG * HEAD_DIM)
    copy = pltpu.make_async_copy(
        slots.at[slot // GANG], target.at[:, here], sems.at[slot // GANG]
    )
    copy.start()
    return [copy]


def causal(tokens):
    rows = lax.broadcasted_iota(jnp.int32, (tokens, tokens), 0)
    cols = lax.broadcasted_iota(jnp.int32, (tokens, tokens), 1)
    return rows >= cols


def key_features_kernel(core, keys, key_out):
    heads_side = key_out.shape[1] // HEAD_DIM
    for place in range(heads_side):
        here = head_columns(side_of(core, False), place, heads_side)
        key_out[:, columns(place)] = feature(keys[:, here].astype(f32)).astype(bf16)


def states_kernel(own, core, keys, values, wire, *key_out):
    heads_side = keys.shape[1] // HEAD_DIM // (CORES if own else 1)
    for place in range(heads_side):
        here = head_columns(side_of(core, own), place, heads_side)
        if own:
            key = feature(keys[:, here].astype(f32)).astype(bf16)
            key_out[0][:, columns(place)] = key
        else:
            key = keys[:, columns(place)]
        row = jnp.sum(key.astype(f32), axis=0, keepdims=True)
        put_state(wire, place, dot(values[:, here], key, 0, 0), row)


def inside_forward_kernel(own, core, queries, values, key_feat, query_out, low_out, numer, denom):
    tokens = queries.shape[0]
    heads_side = key_feat.shape[1] // HEAD_DIM
    mask = causal(tokens)
    for place in range(heads_side):
        here = head_columns(side_of(core, own), place, heads_side)
        there = columns(place)
        query_feat = feature(queries[:, here].astype(f32)).astype(bf16)
        query_out[:, there] = query_feat
        scores = jnp.where(mask, dot(query_feat, key_feat[:, there], 1, 1), 0.0)
        scores_low = scores.astype(bf16)
        low_out[:, columns(place, tokens)] = scores_low
        numer[:, there] = dot(scores_low, values[:, here], 1, 0)
        total = jnp.sum(scores, axis=1, keepdims=True)
        denom[:, there] = jnp.broadcast_to(total, (tokens, HEAD_DIM))


def prepare_kernel(core, queries, keys, gain, out_grad, *outs):
    heads_side = queries.shape[1] // HEAD_DIM // CORES
    for half, own in enumerate((True, False)):
        grad_in, query_slope, key_slope = outs[3 * half : 3 * half + 3]
        for place in range(heads_side):
            here = head_columns(side_of(core, own), place, heads_side)
            there = columns(place)
            grad_in[:, there] = gain[:, here] * out_grad[:, here].astype(f32)
            query_slope[:, there] = feature_slope(queries[:, here].astype(f32))
            key_slope[:, there] = feature_slope(keys[:, here].astype(f32))


def attention_kernel(own, query_feat, numer_in, denom_in, wire, grad_in, *rest):
    tokens, width = query_feat.shape
    heads_side = width // HEAD_DIM
    if own:
        attn_out, inverse_out, squares_out, cross_out = rest
        squares = jnp.zeros((tokens, HEAD_DIM), f32)
        cross = jnp.zeros((tokens, HEAD_DIM), f32)
    else:
        squares_in, cross_in, attn_out, inverse_out, stats = rest
        squares = squares_in[...]
        cross = cross_in[...]
    for place in range(heads_side):
        there = columns(place)
        state, row = get_state(wire, place)
        both = jnp.concatenate([state, jnp.broadcast_to(row, state.shape)], axis=0)
        right = jnp.concatenate(split(both), axis=1)
        query = query_feat[:, there]
        product = dot(jnp.concatenate([query, query], axis=1), right, 1, 1)
        numer = numer_in[:, there] + product[:, :HEAD_DIM]
        inverse = 1.0 / (denom_in[:, there] + product[:, HEAD_DIM:])
        attn = numer * inverse
        squares = squares + attn * attn
        cross = cross + attn * grad_in[:, there]
        attn_out[:, there] = attn
        inverse_out[:, there] = inverse
    if own:
        squares_out[...] = squares
        cross_out[...] = cross
    else:
        ones = jnp.ones((8, 3 * HEAD_DIM), bf16)
        which = lax.broadcasted_iota(jnp.int32, (8, tokens), 0)
        row_squares = dot(ones, parts_of(squares, 1), 1, 1)
        row_cross = dot(ones, parts_of(cross, 1), 1, 1)
        stats[...] = jnp.where(which == 0, row_squares, jnp.where(which == 1, row_cross, 0.0))


def token_scales(stats, width_all):
    tokens = stats.shape[1]
    squares = stats[0:1, :]
    cross = stats[1:2, :]
    scale = lax.rsqrt(squares / width_all + 1e-06)
    slope = scale * scale * scale * (cross / width_all)
    which = lax.broadcasted_iota(jnp.int32, (8, tokens), 0)
    rows = jnp.where(which == 0, scale, jnp.where(which == 1, slope, 0.0))
    pick = lax.broadcasted_iota(jnp.int32, (24, 2 * HEAD_DIM), 0) % 8 == (
        lax.broadcasted_iota(jnp.int32, (24, 2 * HEAD_DIM), 1) // HEAD_DIM
    )
    spread = dot(parts_of(rows, 0), pick.astype(f32).astype(bf16), 0, 0)
    return spread[:, :HEAD_DIM], spread[:, HEAD_DIM:]


def gradient_kernel(own, query_feat, attn_in, inverse_in, grad_in, *rest):
    width = query_feat.shape[1]
    heads_side = width // HEAD_DIM
    if own:
        scale_in, slope_in, numer_out, denom_out, wire = rest
        scale = scale_in[...]
        slope = slope_in[...]
    else:
        parts, (numer_out, denom_out, wire, scale_out, slope_out) = rest[:-5], rest[-5:]
        total = (parts[0][...] + parts[1][...]) + (parts[2][...] + parts[3][...])
        scale, slope = token_scales(total, HEADS * HEAD_DIM)
        scale_out[...] = scale
        slope_out[...] = slope
    for place in range(heads_side):
        there = columns(place)
        attn = attn_in[:, there]
        inverse = inverse_in[:, there]
        d_attn = scale * grad_in[:, there] - attn * slope
        d_numer = d_attn * inverse
        total = jnp.sum(d_attn * attn, axis=1, keepdims=True)
        d_denom = -total * inverse
        numer_out[:, there] = d_numer
        denom_out[:, there] = d_denom
        query = query_feat[:, there]
        row = jnp.sum(d_denom * query.astype(f32), axis=0, keepdims=True)
        put_state(wire, place, dot(d_numer.astype(bf16), query, 0, 0), row)


def early_backward_kernel(low_own, numer_own, low_other, numer_other, part_own, part_other):
    tokens = numer_own.shape[0]
    halves = ((low_own, numer_own, part_own), (low_other, numer_other, part_other))
    for low, d_numer, part in halves:
        for place in range(part.shape[1] // HEAD_DIM):
            there = columns(place)
            numer_low = d_numer[:, there].astype(bf16)
            part[:, there] = dot(low[:, columns(place, tokens)], numer_low, 0, 0)


def inside_backward_kernel(core, values, gain, scale_in, *refs):
    halves, refs = (refs[:7], refs[7:14]), refs[14:]
    normed, query_grad, part_own, part_other, normed_slots, query_slots, sems, mixed_slots = refs
    parts = (part_own, part_other)
    tokens, width = values.shape
    heads_side = width // HEAD_DIM // CORES
    mask = causal(tokens)
    scale = scale_in[...]
    copies = []
    for half, own in enumerate((True, False)):
        query_feat, key_feat, query_slope, d_numer_in, d_denom_in, attn, wire = halves[half]
        side = side_of(core, own)
        for place in range(heads_side):
            here = head_columns(side_of(core, own), place, heads_side)
            there = columns(place)
            slot = half * heads_side + place
            out = (gain[:, here] * attn[:, there] * scale).astype(bf16)
            copies += put_out(normed_slots, normed, sems.at[0], slot, side, heads_side, out)
            state, row = get_state(wire, place)
            state_high, state_low = split(state)
            d_denom = d_denom_in[:, there]
            numer_low, numer_rest = split(d_numer_in[:, there])
            mixed = dot(numer_low, values[:, here], 1, 1)
            mixed = mixed + jnp.concatenate([d_denom, d_denom], axis=1)
            mixed_low = jnp.where(mask, mixed, 0.0).astype(bf16)
            mixed_slots[slot] = mixed_low
            left = jnp.concatenate([numer_low, numer_low, numer_rest], axis=1)
            right = jnp.concatenate([state_high, state_low, state_high], axis=0)
            grad = dot(left, right, 1, 0) + d_denom * row
            grad = grad + dot(mixed_low, key_feat[:, there], 1, 0)
            out = (grad * query_slope[:, there]).astype(bf16)
            copies += put_out(query_slots, query_grad, sems.at[1], slot, side, heads_side, out)
    for half in range(CORES):
        query_feat = halves[half][0]
        for place in range(heads_side):
            there = columns(place)
            mixed_low = mixed_slots[half * heads_side + place]
            parts[half][:, there] = dot(mixed_low, query_feat[:, there], 0, 0)
    for copy in copies:
        copy.wait()


def outside_backward_kernel(
    own, core, key_slope, values, key_feat, key_part, value_part, wire, *rest
):
    key_grad, value_grad, key_slots, value_slots, sems = rest[-5:]
    side = side_of(core, own)
    heads_side = key_feat.shape[1] // HEAD_DIM
    copies = []
    for place in range(heads_side):
        here = head_columns(side_of(core, own), place, heads_side)
        there = columns(place)
        state, row = get_state(wire, place)
        high, low = split(state)
        value = values[:, here]
        key = key_feat[:, there]
        grad = dot(
            jnp.concatenate([value, value], axis=1), jnp.concatenate([high, low], axis=0), 1, 0
        )
        grad = grad + row + key_part[:, there]
        out = (grad * key_slope[:, there]).astype(bf16)
        copies += put_out(key_slots, key_grad, sems.at[0], place, side, heads_side, out)
        grad = dot(
            jnp.concatenate([key, key], axis=1), jnp.concatenate([high, low], axis=1), 1, 1
        )
        out = (grad + value_part[:, there]).astype(bf16)
        copies += put_out(value_slots, value_grad, sems.at[1], place, side, heads_side, out)
    for copy in copies:
        copy.wait()


def group_total_kernel(spread, total):
    value = spread[chunk(0), :]
    for chip in range(1, spread.shape[0] // (ROWS + 1)):
        value = value + spread[chunk(chip), :]
    total[...] = value


def chip_sums_kernel(backward, top, spread, other, sums):
    chips = spread.shape[0] // (ROWS + 1)
    inside = top[0] == (0 if backward else TOP - 1)
    total = jnp.where(inside, other[...], 0.0)
    for step in range(chips):
        chip = chips - 1 - step if backward else step
        sums[chunk(chip), :] = total
        if step < chips - 1:
            total = total + spread[chunk(chip), :]


def halves_of(rows, top):
    size = rows // 2
    for half in range(2):
        there = pl.multiple_of(lax.rem(half + top[0], 2) * size, 8)
        yield pl.ds(half * size, size), pl.ds(there, size)


def pair_kernel(top, mine, extra, pair):
    for here, there in halves_of(pair.shape[0], top):
        pair[here, :] = mine[there, :] + extra[there, :]


def finish_kernel(backward, core, top, kept, mine, extra, own, send):
    later = core[0] == (0 if backward else 1)
    for here, there in halves_of(own.shape[0], top):
        own[here, :] = kept[there, :] + jnp.where(later, extra[here, :], 0.0)
        send[here, :] = kept[there, :] + jnp.where(later, 0.0, mine[here, :])


def shaped(shape, dtype):
    return jax.ShapeDtypeStruct(shape, dtype)


def call(
    kernel, name, out_shape, *operands, scalars=(), flops=0, hbm_in=(), hbm_out=(), slots=0,
    vmem=16, aliases=None, scratch=(),
):
    moved = sum(x.size * x.dtype.itemsize for x in operands)
    moved += sum(x.size * x.dtype.itemsize for x in jax.tree.leaves(out_shape))

    def spaces(count, hbm):
        kinds = [pltpu.HBM if place in hbm else pltpu.VMEM for place in range(count)]
        return [pl.BlockSpec(memory_space=kind) for kind in kinds]

    in_specs = spaces(len(operands), hbm_in)
    out_specs = spaces(len(jax.tree.leaves(out_shape)), hbm_out)
    scratch_shapes = []
    if slots:
        scratch_shapes = [pltpu.VMEM((slots // GANG, BLOCK, GANG * HEAD_DIM), bf16)] * 2
        scratch_shapes.append(pltpu.SemaphoreType.DMA((2, slots // GANG)))
    in_specs = [pl.BlockSpec(memory_space=pltpu.SMEM) for _ in scalars] + in_specs
    operands = scalars + operands
    return pl.pallas_call(
        kernel,
        out_shape=out_shape,
        in_specs=in_specs,
        out_specs=tuple(out_specs) if isinstance(out_shape, tuple) else out_specs[0],
        scratch_shapes=scratch_shapes + list(scratch),
        input_output_aliases=aliases or {},
        compiler_params=pltpu.CompilerParams(vmem_limit_bytes=vmem << 20),
        cost_estimate=pl.CostEstimate(flops=flops, bytes_accessed=moved, transcendentals=0),
        name=name,
    )(*operands)


def swap(array, axis):
    return lax.ppermute(array, axis, [(0, 1), (1, 0)])


def swap_pairs(array, axis, order):
    pairs = [(a, b) for a, b in zip(order[::2], order[1::2])]
    return lax.ppermute(array, axis, pairs + [(b, a) for a, b in pairs])


def after(first, *later):
    return lax.optimization_barrier((first, later))


def exchange(flat, chips):
    chunks = flat.reshape(chips, 1, flat.size // chips)
    return lax.all_to_all(chunks, "chip", 0, 0).reshape(flat.shape)


def scan_chips(mine, extra, core, top, backward, inside=None, operands=()):
    wire = shaped(mine.shape, f32)
    chips = lax.axis_size("chip")
    pair = call(pair_kernel, "pair", wire, mine, extra, scalars=(top,))
    spread = exchange(pair, chips)
    total = call(group_total_kernel, "group_total", shaped((ROWS + 1, HEAD_DIM), f32), spread)
    done = ()
    if inside is not None:
        total, operands = after(total, *operands)
    facing = [(chip, chips + (chip + chips // 2) % chips) for chip in range(chips)]
    other = lax.ppermute(total, ("top", "chip"), facing + [(b, a) for a, b in facing])
    if inside is not None:
        done = inside(*operands)
    other, spread, done = lax.optimization_barrier((other, spread, done))
    kernel = functools.partial(chip_sums_kernel, backward)
    sums = call(kernel, "chip_sums", wire, spread, other, scalars=(top,))
    kept = exchange(sums, chips)
    kernel = functools.partial(finish_kernel, backward)
    own, send = call(kernel, "finish", (wire, wire), kept, mine, extra, scalars=(core, top))
    own, (send,) = after(own, send)
    return own, swap(send, "core"), done


def body(queries, key_rows, value_rows, norm_gain, out_grad):
    tokens, width = queries.shape
    heads = width // HEAD_DIM
    heads_side = heads // CORES
    core = lax.axis_index("core").astype(jnp.int32).reshape(1)
    top = lax.axis_index("top").astype(jnp.int32).reshape(1)
    core, top = lax.optimization_barrier((core, top))
    gain = norm_gain.reshape(1, width)
    wire = shaped((lax.axis_size("chip") * (ROWS + 1), HEAD_DIM), f32)
    narrow = shaped((tokens, width), bf16)
    half_low = shaped((tokens, width // CORES), bf16)
    half = shaped((tokens, width // CORES), f32)
    square = shaped((tokens, heads_side * tokens), bf16)
    lanes = shaped((tokens, HEAD_DIM), f32)
    stats_shape = shaped((8, tokens), f32)
    unit = tokens * HEAD_DIM * HEAD_DIM * heads

    def side_call(kernel, name, own, *args, scalars=(core,), **named):
        kernel = functools.partial(kernel, own)
        return call(kernel, name + ("_own" if own else "_other"), *args, scalars=scalars, **named)

    key_other = call(
        key_features_kernel, "key_features", half_low, key_rows, scalars=(core,)
    )
    theirs = side_call(states_kernel, "states", False, wire, key_other, value_rows, flops=unit)
    theirs, (keys, values) = after(theirs, key_rows, value_rows)
    extra = swap(theirs, "core")
    mine, key_own = side_call(
        states_kernel, "states", True, (wire, half_low), keys, values, flops=unit
    )
    halves = (half_low, square, half, half)
    own_kernels = (queries, key_rows, value_rows, key_own, key_other, gain, out_grad)

    def inside_forward_both(queries, keys, values, key_own, key_other, gain, out_grad):
        first = side_call(
            inside_forward_kernel, "inside_forward", True, halves, queries, values, key_own,
            flops=4 * unit,
        )
        second = side_call(
            inside_forward_kernel, "inside_forward", False, halves, queries, values, key_other,
            flops=4 * unit,
        )
        return first, second, call(
            prepare_kernel, "prepare", (half,) * 6, queries, keys, gain, out_grad,
            scalars=(core,), flops=unit,
        )

    kept, got, inside = scan_chips(
        mine, extra, core, top, False, inside_forward_both, own_kernels
    )
    (query_own, low_own, numer, denom), second, prepared = inside
    query_other, low_other, numer_other, denom_other = second
    grad_own, query_slope, key_slope, grad_other, query_slope_other, key_slope_other = prepared
    attn_own, inverse_own, squares, cross = side_call(
        attention_kernel, "attention", True, (half, half, lanes, lanes),
        query_own, numer, denom, kept, grad_own, flops=4 * unit, scalars=(),
    )
    attn_other, inverse_other, stats = side_call(
        attention_kernel, "attention", False, (half, half, stats_shape),
        query_other, numer_other, denom_other, got, grad_other, squares, cross,
        flops=4 * unit, scalars=(),
    )
    stats_from = [
        swap_pairs(stats, "head", order)
        for order in ((0, 1, 2, 3), (1, 2, 3, 0), (0, 2, 1, 3))
    ]
    d_numer_other, d_denom_other, theirs, scale, slope = side_call(
        gradient_kernel, "gradient", False, (half, half, wire, lanes, lanes),
        query_other, attn_other, inverse_other, grad_other, stats, *stats_from,
        flops=unit, scalars=(),
    )
    theirs, (scale, slope) = after(theirs, scale, slope)
    extra = swap(theirs, "core")
    d_numer_own, d_denom_own, mine = side_call(
        gradient_kernel, "gradient", True, (half, half, wire),
        query_own, attn_own, inverse_own, grad_own, scale, slope, flops=unit, scalars=(),
    )

    mine, (d_numer_own,) = after(mine, d_numer_own)
    value_part, value_part_other = call(
        early_backward_kernel, "early_backward", (half, half),
        low_own, d_numer_own, low_other, d_numer_other, flops=4 * unit,
    )
    extra, mine, value_part, value_part_other = lax.optimization_barrier(
        (extra, mine, value_part, value_part_other)
    )

    def inside_backward(*operands):
        return call(
            inside_backward_kernel, "inside_backward", (narrow, narrow, half, half),
            *operands, scalars=(core,), flops=18 * unit, hbm_out=(0, 1), slots=heads,
            scratch=(pltpu.VMEM((heads, tokens, tokens), bf16),),
        )

    operands = (value_rows, gain, scale)
    operands += (query_own, key_own, query_slope, d_numer_own, d_denom_own, attn_own, kept)
    operands += (query_other, key_other, query_slope_other, d_numer_other, d_denom_other)
    operands += (attn_other, got)
    kept, got, inside = scan_chips(mine, extra, core, top, True, inside_backward, operands)
    normed, query_grad, key_part, key_part_other = inside
    last = dict(flops=4 * unit, hbm_out=(0, 1), slots=heads_side)
    key_grad, value_grad = side_call(
        outside_backward_kernel, "outside_backward", True, (narrow, narrow),
        key_slope, value_rows, key_own, key_part, value_part, kept, **last,
    )
    key_grad, value_grad = side_call(
        outside_backward_kernel, "outside_backward", False, (narrow, narrow),
        key_slope_other, value_rows, key_other, key_part_other, value_part_other, got,
        key_grad, value_grad, hbm_in=(6, 7), aliases={7: 0, 8: 1}, **last,
    )
    return (normed, query_grad, key_grad, value_grad)


def solution(mesh):
    devices = mesh.devices
    fine = Mesh(
        devices.reshape(TOP, devices.shape[0] // (TOP * CORES), CORES, devices.shape[1]),
        ("top", "chip", "core", "head"),
    )
    rows = P(("top", "chip", "core"), "head")
    return jax.shard_map(
        body,
        mesh=fine,
        in_specs=(rows, rows, rows, P("head"), rows),
        out_specs=(rows, rows, rows, rows),
        check_vma=False,
    )
```

```python
import functools

import jax
import jax.numpy as jnp
from jax import lax
from jax.experimental import pallas as pl
from jax.experimental.pallas import tpu as pltpu
from jax.sharding import Mesh
from jax.sharding import PartitionSpec as P

HEADS = 32
HEAD_DIM = 128
CORES = 2
TOP = 2
ROWS = 32
BLOCK = 256
GANG = 2
BLOCKS = HEAD_DIM // ROWS

f32 = jnp.float32
bf16 = jnp.bfloat16


def feature(values):
    return jnp.where(values > 0, values + 1.0, jnp.exp(jnp.minimum(values, 0.0)))


def feature_slope(values):
    return jnp.where(values > 0, jnp.ones_like(values), jnp.exp(jnp.minimum(values, 0.0)))


def dot(left, right, left_dim, right_dim):
    return lax.dot_general(
        left,
        right,
        (((left_dim,), (right_dim,)), ((), ())),
        preferred_element_type=f32,
    )


def split(values):
    high = values.astype(bf16)
    return high, (values - high.astype(f32)).astype(bf16)


def side_of(core, own):
    return core[0] if own else 1 - core[0]


def parts_of(values, axis):
    high, rest = split(values)
    middle = values - high.astype(f32)
    low = (middle - rest.astype(f32)).astype(bf16)
    return jnp.concatenate([high, rest, low], axis=axis)


def head_columns(side, place, heads_side):
    return pl.ds(pl.multiple_of((side * heads_side + place) * HEAD_DIM, HEAD_DIM), HEAD_DIM)


def columns(place, size=HEAD_DIM):
    return pl.ds(place * size, size)


def chunk(place, first=0, size=ROWS + 1):
    return pl.ds(place * (ROWS + 1) + first, size)


def put_state(wire, place, state, row):
    for block in range(BLOCKS):
        here = place * BLOCKS + block
        wire[chunk(here, 0, ROWS), :] = state[block * ROWS : (block + 1) * ROWS]
        wire[chunk(here, ROWS, 1), :] = jnp.zeros_like(row) if block else row


def get_state(wire, place):
    blocks = [wire[chunk(place * BLOCKS + block, 0, ROWS), :] for block in range(BLOCKS)]
    return jnp.concatenate(blocks, axis=0), wire[chunk(place * BLOCKS, ROWS, 1), :]


def put_out(slots, target, sems, slot, side, heads_side, value):
    place = slot % GANG
    slots[slot // GANG, :, columns(place)] = value
    if place != GANG - 1:
        return []
    first = (side * heads_side + slot % heads_side - place) * HEAD_DIM
    here = pl.ds(pl.multiple_of(first, HEAD_DIM), GANG * HEAD_DIM)
    copy = pltpu.make_async_copy(
        slots.at[slot // GANG], target.at[:, here], sems.at[slot // GANG]
    )
    copy.start()
    return [copy]


def causal(tokens):
    rows = lax.broadcasted_iota(jnp.int32, (tokens, tokens), 0)
    cols = lax.broadcasted_iota(jnp.int32, (tokens, tokens), 1)
    return rows >= cols


def key_features_kernel(core, keys, key_out):
    heads_side = key_out.shape[1] // HEAD_DIM
    for place in range(heads_side):
        here = head_columns(side_of(core, False), place, heads_side)
        key_out[:, columns(place)] = feature(keys[:, here].astype(f32)).astype(bf16)


def states_kernel(own, core, keys, values, wire, *key_out):
    heads_side = keys.shape[1] // HEAD_DIM // (CORES if own else 1)
    for place in range(heads_side):
        here = head_columns(side_of(core, own), place, heads_side)
        if own:
            key = feature(keys[:, here].astype(f32)).astype(bf16)
            key_out[0][:, columns(place)] = key
        else:
            key = keys[:, columns(place)]
        row = jnp.sum(key.astype(f32), axis=0, keepdims=True)
        put_state(wire, place, dot(values[:, here], key, 0, 0), row)


def inside_forward_kernel(own, core, queries, values, key_feat, query_out, low_out, numer, denom):
    tokens = queries.shape[0]
    heads_side = key_feat.shape[1] // HEAD_DIM
    mask = causal(tokens)
    for place in range(heads_side):
        here = head_columns(side_of(core, own), place, heads_side)
        there = columns(place)
        query_feat = feature(queries[:, here].astype(f32)).astype(bf16)
        query_out[:, there] = query_feat
        scores = jnp.where(mask, dot(query_feat, key_feat[:, there], 1, 1), 0.0)
        scores_low = scores.astype(bf16)
        low_out[:, columns(place, tokens)] = scores_low
        numer[:, there] = dot(scores_low, values[:, here], 1, 0)
        total = jnp.sum(scores, axis=1, keepdims=True)
        denom[:, there] = jnp.broadcast_to(total, (tokens, HEAD_DIM))


def prepare_kernel(core, queries, keys, gain, out_grad, *outs):
    heads_side = queries.shape[1] // HEAD_DIM // CORES
    for half, own in enumerate((True, False)):
        grad_in, query_slope, key_slope = outs[3 * half : 3 * half + 3]
        for place in range(heads_side):
            here = head_columns(side_of(core, own), place, heads_side)
            there = columns(place)
            grad_in[:, there] = gain[:, here] * out_grad[:, here].astype(f32)
            query_slope[:, there] = feature_slope(queries[:, here].astype(f32))
            key_slope[:, there] = feature_slope(keys[:, here].astype(f32))


def attention_kernel(own, query_feat, numer_in, denom_in, wire, grad_in, *rest):
    tokens, width = query_feat.shape
    heads_side = width // HEAD_DIM
    if own:
        attn_out, inverse_out, squares_out, cross_out = rest
        squares = jnp.zeros((tokens, HEAD_DIM), f32)
        cross = jnp.zeros((tokens, HEAD_DIM), f32)
    else:
        squares_in, cross_in, attn_out, inverse_out, stats = rest
        squares = squares_in[...]
        cross = cross_in[...]
    for place in range(heads_side):
        there = columns(place)
        state, row = get_state(wire, place)
        both = jnp.concatenate([state, jnp.broadcast_to(row, state.shape)], axis=0)
        right = jnp.concatenate(split(both), axis=1)
        query = query_feat[:, there]
        product = dot(jnp.concatenate([query, query], axis=1), right, 1, 1)
        numer = numer_in[:, there] + product[:, :HEAD_DIM]
        inverse = 1.0 / (denom_in[:, there] + product[:, HEAD_DIM:])
        attn = numer * inverse
        squares = squares + attn * attn
        cross = cross + attn * grad_in[:, there]
        attn_out[:, there] = attn
        inverse_out[:, there] = inverse
    if own:
        squares_out[...] = squares
        cross_out[...] = cross
    else:
        ones = jnp.ones((8, 3 * HEAD_DIM), bf16)
        which = lax.broadcasted_iota(jnp.int32, (8, tokens), 0)
        row_squares = dot(ones, parts_of(squares, 1), 1, 1)
        row_cross = dot(ones, parts_of(cross, 1), 1, 1)
        stats[...] = jnp.where(which == 0, row_squares, jnp.where(which == 1, row_cross, 0.0))


def token_scales(stats, width_all):
    tokens = stats.shape[1]
    squares = stats[0:1, :]
    cross = stats[1:2, :]
    scale = lax.rsqrt(squares / width_all + 1e-06)
    slope = scale * scale * scale * (cross / width_all)
    which = lax.broadcasted_iota(jnp.int32, (8, tokens), 0)
    rows = jnp.where(which == 0, scale, jnp.where(which == 1, slope, 0.0))
    pick = lax.broadcasted_iota(jnp.int32, (24, 2 * HEAD_DIM), 0) % 8 == (
        lax.broadcasted_iota(jnp.int32, (24, 2 * HEAD_DIM), 1) // HEAD_DIM
    )
    spread = dot(parts_of(rows, 0), pick.astype(f32).astype(bf16), 0, 0)
    return spread[:, :HEAD_DIM], spread[:, HEAD_DIM:]


def gradient_kernel(own, query_feat, attn_in, inverse_in, grad_in, *rest):
    width = query_feat.shape[1]
    heads_side = width // HEAD_DIM
    if own:
        scale_in, slope_in, numer_out, denom_out, wire = rest
        scale = scale_in[...]
        slope = slope_in[...]
    else:
        parts, (numer_out, denom_out, wire, scale_out, slope_out) = rest[:-5], rest[-5:]
        total = (parts[0][...] + parts[1][...]) + (parts[2][...] + parts[3][...])
        scale, slope = token_scales(total, HEADS * HEAD_DIM)
        scale_out[...] = scale
        slope_out[...] = slope
    for place in range(heads_side):
        there = columns(place)
        attn = attn_in[:, there]
        inverse = inverse_in[:, there]
        d_attn = scale * grad_in[:, there] - attn * slope
        d_numer = d_attn * inverse
        total = jnp.sum(d_attn * attn, axis=1, keepdims=True)
        d_denom = -total * inverse
        numer_out[:, there] = d_numer
        denom_out[:, there] = d_denom
        query = query_feat[:, there]
        row = jnp.sum(d_denom * query.astype(f32), axis=0, keepdims=True)
        put_state(wire, place, dot(d_numer.astype(bf16), query, 0, 0), row)


def early_backward_kernel(low_own, numer_own, low_other, numer_other, part_own, part_other):
    tokens = numer_own.shape[0]
    halves = ((low_own, numer_own, part_own), (low_other, numer_other, part_other))
    for low, d_numer, part in halves:
        for place in range(part.shape[1] // HEAD_DIM):
            there = columns(place)
            numer_low = d_numer[:, there].astype(bf16)
            part[:, there] = dot(low[:, columns(place, tokens)], numer_low, 0, 0)


def inside_backward_kernel(core, values, gain, scale_in, *refs):
    halves, refs = (refs[:7], refs[7:14]), refs[14:]
    normed, query_grad, part_own, part_other, normed_slots, query_slots, sems, mixed_slots = refs
    parts = (part_own, part_other)
    tokens, width = values.shape
    heads_side = width // HEAD_DIM // CORES
    mask = causal(tokens)
    scale = scale_in[...]
    copies = []
    for half, own in enumerate((True, False)):
        query_feat, key_feat, query_slope, d_numer_in, d_denom_in, attn, wire = halves[half]
        side = side_of(core, own)
        for place in range(heads_side):
            here = head_columns(side_of(core, own), place, heads_side)
            there = columns(place)
            slot = half * heads_side + place
            out = (gain[:, here] * attn[:, there] * scale).astype(bf16)
            copies += put_out(normed_slots, normed, sems.at[0], slot, side, heads_side, out)
            state, row = get_state(wire, place)
            state_high, state_low = split(state)
            d_denom = d_denom_in[:, there]
            numer_low, numer_rest = split(d_numer_in[:, there])
            mixed = dot(numer_low, values[:, here], 1, 1)
            mixed = mixed + jnp.concatenate([d_denom, d_denom], axis=1)
            mixed_low = jnp.where(mask, mixed, 0.0).astype(bf16)
            mixed_slots[slot] = mixed_low
            left = jnp.concatenate([numer_low, numer_low, numer_rest], axis=1)
            right = jnp.concatenate([state_high, state_low, state_high], axis=0)
            grad = dot(left, right, 1, 0) + d_denom * row
            grad = grad + dot(mixed_low, key_feat[:, there], 1, 0)
            out = (grad * query_slope[:, there]).astype(bf16)
            copies += put_out(query_slots, query_grad, sems.at[1], slot, side, heads_side, out)
    for half in range(CORES):
        query_feat = halves[half][0]
        for place in range(heads_side):
            there = columns(place)
            mixed_low = mixed_slots[half * heads_side + place]
            parts[half][:, there] = dot(mixed_low, query_feat[:, there], 0, 0)
    for copy in copies:
        copy.wait()


def outside_backward_kernel(
    own, core, key_slope, values, key_feat, key_part, value_part, wire, *rest
):
    key_grad, value_grad, key_slots, value_slots, sems = rest[-5:]
    side = side_of(core, own)
    heads_side = key_feat.shape[1] // HEAD_DIM
    copies = []
    for place in range(heads_side):
        here = head_columns(side_of(core, own), place, heads_side)
        there = columns(place)
        state, row = get_state(wire, place)
        high, low = split(state)
        value = values[:, here]
        key = key_feat[:, there]
        grad = dot(
            jnp.concatenate([value, value], axis=1), jnp.concatenate([high, low], axis=0), 1, 0
        )
        grad = grad + row + key_part[:, there]
        out = (grad * key_slope[:, there]).astype(bf16)
        copies += put_out(key_slots, key_grad, sems.at[0], place, side, heads_side, out)
        grad = dot(
            jnp.concatenate([key, key], axis=1), jnp.concatenate([high, low], axis=1), 1, 1
        )
        out = (grad + value_part[:, there]).astype(bf16)
        copies += put_out(value_slots, value_grad, sems.at[1], place, side, heads_side, out)
    for copy in copies:
        copy.wait()


def group_total_kernel(spread, total):
    value = spread[chunk(0), :]
    for chip in range(1, spread.shape[0] // (ROWS + 1)):
        value = value + spread[chunk(chip), :]
    total[...] = value


def chip_sums_kernel(backward, top, spread, other, sums):
    chips = spread.shape[0] // (ROWS + 1)
    inside = top[0] == (0 if backward else TOP - 1)
    total = jnp.where(inside, other[...], 0.0)
    for step in range(chips):
        chip = chips - 1 - step if backward else step
        sums[chunk(chip), :] = total
        if step < chips - 1:
            total = total + spread[chunk(chip), :]


def halves_of(rows, top):
    size = rows // 2
    for half in range(2):
        there = pl.multiple_of(lax.rem(half + top[0], 2) * size, 8)
        yield pl.ds(half * size, size), pl.ds(there, size)


def pair_kernel(top, mine, extra, pair):
    for here, there in halves_of(pair.shape[0], top):
        pair[here, :] = mine[there, :] + extra[there, :]


def finish_kernel(backward, core, top, kept, mine, extra, own, send):
    later = core[0] == (0 if backward else 1)
    for here, there in halves_of(own.shape[0], top):
        own[here, :] = kept[there, :] + jnp.where(later, extra[here, :], 0.0)
        send[here, :] = kept[there, :] + jnp.where(later, 0.0, mine[here, :])


def shaped(shape, dtype):
    return jax.ShapeDtypeStruct(shape, dtype)


def call(
    kernel, name, out_shape, *operands, scalars=(), flops=0, hbm_in=(), hbm_out=(), slots=0,
    vmem=16, aliases=None, scratch=(),
):
    moved = sum(x.size * x.dtype.itemsize for x in operands)
    moved += sum(x.size * x.dtype.itemsize for x in jax.tree.leaves(out_shape))

    def spaces(count, hbm):
        kinds = [pltpu.HBM if place in hbm else pltpu.VMEM for place in range(count)]
        return [pl.BlockSpec(memory_space=kind) for kind in kinds]

    in_specs = spaces(len(operands), hbm_in)
    out_specs = spaces(len(jax.tree.leaves(out_shape)), hbm_out)
    scratch_shapes = []
    if slots:
        scratch_shapes = [pltpu.VMEM((slots // GANG, BLOCK, GANG * HEAD_DIM), bf16)] * 2
        scratch_shapes.append(pltpu.SemaphoreType.DMA((2, slots // GANG)))
    in_specs = [pl.BlockSpec(memory_space=pltpu.SMEM) for _ in scalars] + in_specs
    operands = scalars + operands
    return pl.pallas_call(
        kernel,
        out_shape=out_shape,
        in_specs=in_specs,
        out_specs=tuple(out_specs) if isinstance(out_shape, tuple) else out_specs[0],
        scratch_shapes=scratch_shapes + list(scratch),
        input_output_aliases=aliases or {},
        compiler_params=pltpu.CompilerParams(vmem_limit_bytes=vmem << 20),
        cost_estimate=pl.CostEstimate(flops=flops, bytes_accessed=moved, transcendentals=0),
        name=name,
    )(*operands)


def swap(array, axis):
    return lax.ppermute(array, axis, [(0, 1), (1, 0)])


def swap_pairs(array, axis, order):
    pairs = [(a, b) for a, b in zip(order[::2], order[1::2])]
    return lax.ppermute(array, axis, pairs + [(b, a) for a, b in pairs])


def after(first, *later):
    return lax.optimization_barrier((first, later))


def exchange(flat, chips):
    chunks = flat.reshape(chips, 1, flat.size // chips)
    return lax.all_to_all(chunks, "chip", 0, 0).reshape(flat.shape)


def scan_chips(mine, extra, core, top, backward, inside=None, operands=()):
    wire = shaped(mine.shape, f32)
    chips = lax.axis_size("chip")
    pair = call(pair_kernel, "pair", wire, mine, extra, scalars=(top,))
    spread = exchange(pair, chips)
    total = call(group_total_kernel, "group_total", shaped((ROWS + 1, HEAD_DIM), f32), spread)
    done = ()
    if inside is not None:
        total, operands = after(total, *operands)
    facing = [(chip, chips + (chip + chips // 2) % chips) for chip in range(chips)]
    other = lax.ppermute(total, ("top", "chip"), facing + [(b, a) for a, b in facing])
    if inside is not None:
        done = inside(*operands)
    other, spread, done = lax.optimization_barrier((other, spread, done))
    kernel = functools.partial(chip_sums_kernel, backward)
    sums = call(kernel, "chip_sums", wire, spread, other, scalars=(top,))
    kept = exchange(sums, chips)
    kernel = functools.partial(finish_kernel, backward)
    own, send = call(kernel, "finish", (wire, wire), kept, mine, extra, scalars=(core, top))
    own, (send,) = after(own, send)
    return own, swap(send, "core"), done


def body(queries, key_rows, value_rows, norm_gain, out_grad):
    tokens, width = queries.shape
    heads = width // HEAD_DIM
    heads_side = heads // CORES
    core = lax.axis_index("core").astype(jnp.int32).reshape(1)
    top = lax.axis_index("top").astype(jnp.int32).reshape(1)
    core, top = lax.optimization_barrier((core, top))
    gain = norm_gain.reshape(1, width)
    wire = shaped((lax.axis_size("chip") * (ROWS + 1), HEAD_DIM), f32)
    narrow = shaped((tokens, width), bf16)
    half_low = shaped((tokens, width // CORES), bf16)
    half = shaped((tokens, width // CORES), f32)
    square = shaped((tokens, heads_side * tokens), bf16)
    lanes = shaped((tokens, HEAD_DIM), f32)
    stats_shape = shaped((8, tokens), f32)
    unit = tokens * HEAD_DIM * HEAD_DIM * heads

    def side_call(kernel, name, own, *args, scalars=(core,), **named):
        kernel = functools.partial(kernel, own)
        return call(kernel, name + ("_own" if own else "_other"), *args, scalars=scalars, **named)

    key_other = call(
        key_features_kernel, "key_features", half_low, key_rows, scalars=(core,)
    )
    theirs = side_call(states_kernel, "states", False, wire, key_other, value_rows, flops=unit)
    theirs, (keys, values) = after(theirs, key_rows, value_rows)
    extra = swap(theirs, "core")
    mine, key_own = side_call(
        states_kernel, "states", True, (wire, half_low), keys, values, flops=unit
    )
    halves = (half_low, square, half, half)
    own_kernels = (queries, key_rows, value_rows, key_own, gain, out_grad)

    def inside_forward_own(queries, keys, values, key_own, gain, out_grad):
        first = side_call(
            inside_forward_kernel, "inside_forward", True, halves, queries, values, key_own,
            flops=4 * unit,
        )
        return first, call(
            prepare_kernel, "prepare", (half,) * 6, queries, keys, gain, out_grad,
            scalars=(core,), flops=unit,
        )

    kept, got, inside = scan_chips(
        mine, extra, core, top, False, inside_forward_own, own_kernels
    )
    (query_own, low_own, numer, denom), prepared = inside
    grad_own, query_slope, key_slope, grad_other, query_slope_other, key_slope_other = prepared
    kept, (key_other,) = after(kept, key_other)
    query_other, low_other, numer_other, denom_other = side_call(
        inside_forward_kernel, "inside_forward", False, halves, queries, value_rows, key_other,
        flops=4 * unit,
    )
    attn_own, inverse_own, squares, cross = side_call(
        attention_kernel, "attention", True, (half, half, lanes, lanes),
        query_own, numer, denom, kept, grad_own, flops=4 * unit, scalars=(),
    )
    attn_other, inverse_other, stats = side_call(
        attention_kernel, "attention", False, (half, half, stats_shape),
        query_other, numer_other, denom_other, got, grad_other, squares, cross,
        flops=4 * unit, scalars=(),
    )
    stats_from = [
        swap_pairs(stats, "head", order)
        for order in ((0, 1, 2, 3), (1, 2, 3, 0), (0, 2, 1, 3))
    ]
    d_numer_other, d_denom_other, theirs, scale, slope = side_call(
        gradient_kernel, "gradient", False, (half, half, wire, lanes, lanes),
        query_other, attn_other, inverse_other, grad_other, stats, *stats_from,
        flops=unit, scalars=(),
    )
    theirs, (scale, slope) = after(theirs, scale, slope)
    extra = swap(theirs, "core")
    d_numer_own, d_denom_own, mine = side_call(
        gradient_kernel, "gradient", True, (half, half, wire),
        query_own, attn_own, inverse_own, grad_own, scale, slope, flops=unit, scalars=(),
    )

    mine, (d_numer_own,) = after(mine, d_numer_own)
    value_part, value_part_other = call(
        early_backward_kernel, "early_backward", (half, half),
        low_own, d_numer_own, low_other, d_numer_other, flops=4 * unit,
    )
    extra, mine, value_part, value_part_other = lax.optimization_barrier(
        (extra, mine, value_part, value_part_other)
    )

    def inside_backward(*operands):
        return call(
            inside_backward_kernel, "inside_backward", (narrow, narrow, half, half),
            *operands, scalars=(core,), flops=18 * unit, hbm_out=(0, 1), slots=heads,
            scratch=(pltpu.VMEM((heads, tokens, tokens), bf16),),
        )

    operands = (value_rows, gain, scale)
    operands += (query_own, key_own, query_slope, d_numer_own, d_denom_own, attn_own, kept)
    operands += (query_other, key_other, query_slope_other, d_numer_other, d_denom_other)
    operands += (attn_other, got)
    kept, got, inside = scan_chips(mine, extra, core, top, True, inside_backward, operands)
    normed, query_grad, key_part, key_part_other = inside
    last = dict(flops=4 * unit, hbm_out=(0, 1), slots=heads_side)
    key_grad, value_grad = side_call(
        outside_backward_kernel, "outside_backward", True, (narrow, narrow),
        key_slope, value_rows, key_own, key_part, value_part, kept, **last,
    )
    key_grad, value_grad = side_call(
        outside_backward_kernel, "outside_backward", False, (narrow, narrow),
        key_slope_other, value_rows, key_other, key_part_other, value_part_other, got,
        key_grad, value_grad, hbm_in=(6, 7), aliases={7: 0, 8: 1}, **last,
    )
    return (normed, query_grad, key_grad, value_grad)


def solution(mesh):
    devices = mesh.devices
    fine = Mesh(
        devices.reshape(TOP, devices.shape[0] // (TOP * CORES), CORES, devices.shape[1]),
        ("top", "chip", "core", "head"),
    )
    rows = P(("top", "chip", "core"), "head")
    return jax.shard_map(
        body,
        mesh=fine,
        in_specs=(rows, rows, rows, P("head"), rows),
        out_specs=(rows, rows, rows, rows),
        check_vma=False,
    )
```
